256 devices in a mesh: col: 16 (over z, core), sec: 16 (over y, x).
Axes of the slice: x: 4, y: 4, z: 8, core: 2. Of those that a mesh axis runs over, the one named last changes fastest.
Arguments:
- env_right: bfloat16 [1, 65536, 128], P(None, 'sec'), may hold values from -6 to 6
- transfer: bfloat16 [16, 1, 65536, 4, 128], P('col', None, 'sec'), may hold values from -0.25 to 0.25
- sources: int32 [16, 1, 512, 4], P('col', None, 'sec'), may hold values from 0 to 511, as said below
- env_left: bfloat16 [16, 1, 65536, 128], P('col', None, 'sec'), may hold values from -0.5 to 0.5
Outputs:
- env_out: bfloat16 [16, 1, 65536, 128], P('col', None, 'sec')
- grad: bfloat16 [16, 1, 65536, 4, 128], P('col', None, 'sec')
The draws below stay inside these ranges and needn't reach their ends.
Inputs may be any that keep to these rules, and one draw needn't show every extreme that they name: `sources`: every source tile lies within 2 tiles of its output tile; each list holds the tiles at offsets -2 and +2 (reflected at the ends of the space) and two of the offsets -1, 0, 1.
All inputs are finite; a program needn't handle non-finite values.
Results may differ from the reference program's by a relative error of at most 0.029.
Values may be sent and summed in bfloat16 or wider, within the bound.
A program may use at most 64 MiB of HBM per device.

```python
import jax
import jax.numpy as jnp

K = 128
TILE = 128
PAIRS = 4
REACH = 2
ROWS = 1
NCOLS = 16
NT = 512
F = 65536


def draw_sources(key, part):
    dropped = jax.random.randint(key, (NCOLS, ROWS, NT), 0, 3)
    below = jnp.where(dropped == 0, 0, -1).astype(jnp.int32)
    above = jnp.where(dropped == 2, 0, 1).astype(jnp.int32)
    distant = jnp.full((NCOLS, ROWS, NT), REACH, jnp.int32)
    offsets = jnp.stack([-distant, distant, below, above], axis=-1)
    tile_index = jnp.arange(NT, dtype=jnp.int32)[None, None, :, None]
    source_tile = tile_index + offsets
    source_tile = jnp.where(source_tile < 0, -source_tile, source_tile)
    source_tile = jnp.where(source_tile > NT - 1, 2 * (NT - 1) - source_tile, source_tile)
    return source_tile.astype(jnp.int32)


def shard_levels(rng, dims, pieces, low, largest):
    factor_of = 1.0
    for dim, blocks in pieces:
        heights = jax.random.uniform(jax.random.fold_in(jax.random.fold_in(rng, 6), dim), (blocks,), jnp.float32, low / len(pieces), largest / len(pieces))
        factor_of = factor_of * jnp.repeat(jnp.exp(heights), dims[dim] // blocks).reshape((-1,) + (1,) * (len(dims) - 1 - dim))
    return factor_of


def gaussian(key, extent, spread, bound, cuts=(), kind=jnp.bfloat16):
    result = jax.random.normal(key, extent, jnp.float32) * spread
    if len(cuts) > 0:
        result = shard_levels(key, extent, cuts, -0.22, 0.18) * result
    return jnp.clip(result, min=-bound, max=bound).astype(kind)


def setup_inputs(seed: int = 0) -> dict:
    arg_keys = jax.random.split(jax.random.key(seed), 5)
    return {
        "env_right": gaussian(arg_keys[0], (ROWS, F, K), 1.0, 6.0, ((1, 16),)),
        "transfer": gaussian(arg_keys[1], (NCOLS, ROWS, F, PAIRS, TILE), (PAIRS * TILE) ** -0.5, 0.25, ((0, 16), (2, 16))),
        "sources": draw_sources(jax.random.fold_in(arg_keys[4], 71), 0),
        "env_left": gaussian(arg_keys[3], (NCOLS, ROWS, F, K), K ** -0.5, 0.5, ((0, 16), (2, 16))),
    }


def pick_blocks(state, source_list):
    blocks = state.reshape(ROWS, NT, TILE, K)

    def one_row(row_blocks, row_sources):
        return row_blocks[row_sources]

    return jax.vmap(one_row)(blocks, source_list)


def reference(env_right, transfer, sources, env_left):
    state = env_right
    env_list = []
    grad_list = []
    for column in reversed(range(NCOLS)):
        picked = pick_blocks(state, sources[column]).astype(jnp.float32)
        blocks = transfer[column].reshape(ROWS, NT, TILE, PAIRS, TILE).astype(jnp.float32)
        fresh = jnp.einsum('rtopq,rtpqk->rtok', blocks, picked)
        fresh = fresh.reshape(ROWS, F, K).astype(jnp.bfloat16)
        left = env_left[column].reshape(ROWS, NT, TILE, K).astype(jnp.float32)
        block_grad = jnp.einsum('rtok,rtpqk->rtopq', left, picked)
        grad_list.append(block_grad.reshape(ROWS, F, PAIRS, TILE).astype(jnp.bfloat16))
        env_list.append(fresh)
        state = fresh
    env_out = jnp.stack(env_list[::-1], axis=0)
    grad = jnp.stack(grad_list[::-1], axis=0)
    return env_out, grad
```

```python
import functools

import jax
import jax.numpy as jnp
from jax import lax
from jax.experimental import pallas as pl
from jax.experimental.pallas import tpu as pltpu
from jax.sharding import PartitionSpec as P

TILE = 128
REACH = 2
CHUNK = REACH * TILE
MESH = pl.DeviceIdType.MESH


def sweep_kernel(
    ncol, nsec, src_ref, env_hbm, a_hbm, left_hbm, env_out, grad_out,
    a_v, left_v, land, win, fresh, grad_v,
    recv_sem, send_sem, a_sem, left_sem, out_sem, gout_sem,
):
    col = lax.axis_index("col")
    sec = lax.axis_index("sec")
    chunks = a_v.shape[0] // CHUNK
    tiles = a_v.shape[0] // TILE
    pairs = src_ref.shape[0]
    odd = sec % 2
    first = col == ncol - 1
    has_below = sec > 0
    has_above = sec < nsec - 1

    def place(m):
        return m + odd * (chunks - 1 - 2 * m)

    def slot(m):
        return place(m) + 1

    def rows(q):
        return pl.ds(pl.multiple_of(q * CHUNK, CHUNK), CHUNK)

    def exists(w):
        return jnp.logical_and(jnp.logical_or(w > 0, has_below), jnp.logical_or(w <= chunks, has_above))

    def arrival(w):
        return pltpu.make_async_copy(land.at[rows(w)], land.at[rows(w)], recv_sem.at[w])

    def load_a(q):
        return pltpu.make_async_copy(a_hbm.at[rows(q)], a_v.at[rows(q)], a_sem.at[q])

    def load_left(q):
        return pltpu.make_async_copy(left_hbm.at[rows(q)], left_v.at[rows(q)], left_sem.at[q])

    def load_env(q):
        return pltpu.make_async_copy(env_hbm.at[rows(q)], land.at[rows(q + 1)], recv_sem.at[q + 1])

    def store_env(q):
        return pltpu.make_async_copy(fresh.at[rows(q)], env_out.at[rows(q)], out_sem.at[q])

    def store_grad(q):
        return pltpu.make_async_copy(grad_v.at[rows(q)], grad_out.at[rows(q)], gout_sem.at[q])

    def send(src, q, w, sem, to_col, to_sec):
        return pltpu.make_async_remote_copy(
            src_ref=src.at[rows(q)],
            dst_ref=land.at[rows(w)],
            send_sem=send_sem.at[sem],
            recv_sem=recv_sem.at[w],
            device_id=(to_col, to_sec),
            device_id_type=MESH,
        )

    barrier = pltpu.get_barrier_semaphore()

    def greet(to_col, to_sec):
        pl.semaphore_signal(barrier, inc=1, device_id=(to_col, to_sec), device_id_type=MESH)

    @pl.when(jnp.logical_not(first))
    def _():
        greet(col + 1, sec)

        @pl.when(has_below)
        def _():
            greet(col + 1, sec - 1)

        @pl.when(has_above)
        def _():
            greet(col + 1, sec + 1)

    @pl.when(first)
    def _():
        @pl.when(has_below)
        def _():
            greet(col, sec - 1)

        @pl.when(has_above)
        def _():
            greet(col, sec + 1)

    def start_loads(m, carry):
        q = place(m)

        @pl.when(first)
        def _():
            load_env(q).start()

        load_a(q).start()
        load_left(q).start()
        return carry

    lax.fori_loop(0, chunks, start_loads, 0)
    win[...] = jnp.zeros_like(win)

    def count(flag):
        return flag.astype(jnp.int32)

    beside = count(has_below) + count(has_above)

    @pl.when(col > 0)
    def _():
        pl.semaphore_wait(barrier, 1 + beside + count(first) * beside)

    @pl.when(first)
    def _():
        @pl.when(has_below)
        def _():
            send(env_hbm, 0, chunks + 1, chunks + 2, col, sec - 1).start()

        @pl.when(has_above)
        def _():
            send(env_hbm, chunks - 1, 0, chunks + 3, col, sec + 1).start()

    def take(w):
        @pl.when(exists(w))
        def _():
            arrival(w).wait()
            for u in range(REACH):
                win[w * REACH + u] = land[pl.ds(pl.multiple_of(w * CHUNK, CHUNK) + u * TILE, TILE), :]

    take(slot(-1))
    take(slot(0))

    def step(m, carry):
        q = place(m)
        take(slot(m + 1))
        load_a(q).wait()

        def picked(t):
            parts = []
            for j in range(pairs):
                i = src_ref[j, t] - sec * tiles + REACH
                parts.append(win[jnp.clip(i, 0, win.shape[0] - 1)])
            return jnp.concatenate(parts, axis=0)

        def tile_rows(t):
            return pl.ds(pl.multiple_of(t * TILE, TILE), TILE)

        for u in range(REACH):
            t = q * REACH + u
            acc = jnp.dot(a_v[tile_rows(t), :], picked(t), preferred_element_type=jnp.float32)
            fresh[tile_rows(t), :] = acc.astype(jnp.bfloat16)

        @pl.when(col > 0)
        def _():
            send(fresh, q, q + 1, q, col - 1, sec).start()

            @pl.when(jnp.logical_and(q == 0, has_below))
            def _():
                send(fresh, 0, chunks + 1, chunks, col - 1, sec - 1).start()

            @pl.when(jnp.logical_and(q == chunks - 1, has_above))
            def _():
                send(fresh, chunks - 1, 0, chunks + 1, col - 1, sec + 1).start()

        store_env(q).start()
        load_left(q).wait()
        for u in range(REACH):
            t = q * REACH + u
            g = lax.dot_general(
                left_v[tile_rows(t), :], picked(t), (((1,), (1,)), ((), ())), preferred_element_type=jnp.float32
            )
            grad_v[tile_rows(t), :] = g.astype(jnp.bfloat16)
        store_grad(q).start()
        return carry

    lax.fori_loop(0, chunks, step, 0)

    def drain(q, carry):
        store_env(q).wait()
        store_grad(q).wait()

        @pl.when(col > 0)
        def _():
            send(fresh, q, q + 1, q, col - 1, sec).wait_send()

        return carry

    lax.fori_loop(0, chunks, drain, 0)

    @pl.when(jnp.logical_and(col > 0, has_below))
    def _():
        send(fresh, 0, chunks + 1, chunks, col - 1, sec - 1).wait_send()

    @pl.when(jnp.logical_and(col > 0, has_above))
    def _():
        send(fresh, chunks - 1, 0, chunks + 1, col - 1, sec + 1).wait_send()

    @pl.when(jnp.logical_and(first, has_below))
    def _():
        send(env_hbm, 0, chunks + 1, chunks + 2, col, sec - 1).wait_send()

    @pl.when(jnp.logical_and(first, has_above))
    def _():
        send(env_hbm, chunks - 1, 0, chunks + 3, col, sec + 1).wait_send()


def per_device(env_right, transfer, sources, env_left):
    ncol = lax.axis_size("col")
    nsec = lax.axis_size("sec")
    length = transfer.shape[2]
    pairs = transfer.shape[3]
    width = env_right.shape[2]
    chunks = length // CHUNK
    a = transfer.reshape(length, pairs * TILE)
    left = env_left.reshape(length, width)
    src = jnp.transpose(sources.reshape(length // TILE, pairs))
    bf16 = jnp.bfloat16
    anywhere = pl.BlockSpec(memory_space=pl.ANY)
    env, grad = pl.pallas_call(
        functools.partial(sweep_kernel, ncol, nsec),
        out_shape=(
            jax.ShapeDtypeStruct((length, width), bf16),
            jax.ShapeDtypeStruct((length, pairs * TILE), bf16),
        ),
        in_specs=[pl.BlockSpec(memory_space=pltpu.SMEM), anywhere, anywhere, anywhere],
        out_specs=(anywhere, anywhere),
        scratch_shapes=[
            pltpu.VMEM((length, pairs * TILE), bf16),
            pltpu.VMEM((length, width), bf16),
            pltpu.VMEM((length + 2 * CHUNK, width), bf16),
            pltpu.VMEM((length // TILE + 2 * REACH, TILE, width), bf16),
            pltpu.VMEM((length, width), bf16),
            pltpu.VMEM((length, pairs * TILE), bf16),
            pltpu.SemaphoreType.DMA((chunks + 2,)),
            pltpu.SemaphoreType.DMA((chunks + 4,)),
            pltpu.SemaphoreType.DMA((chunks,)),
            pltpu.SemaphoreType.DMA((chunks,)),
            pltpu.SemaphoreType.DMA((chunks,)),
            pltpu.SemaphoreType.DMA((chunks,)),
        ],
        compiler_params=pltpu.CompilerParams(
            collective_id=0, has_side_effects=True, vmem_limit_bytes=24 * 1024 * 1024
        ),
        name="sweep",
    )(src, env_right.reshape(length, width), a, left)
    return env.reshape(1, 1, length, width), grad.reshape(1, 1, length, pairs, TILE)


def solution(mesh):
    placed = (
        P(None, "sec", None),
        P("col", None, "sec", None, None),
        P("col", None, "sec", None),
        P("col", None, "sec", None),
    )
    return jax.shard_map(
        per_device,
        mesh=mesh,
        in_specs=placed,
        out_specs=(P("col", None, "sec", None), P("col", None, "sec", None, None)),
        check_vma=False,
    )
```

```python
import functools

import jax
import jax.numpy as jnp
from jax import lax
from jax.experimental import pallas as pl
from jax.experimental.pallas import tpu as pltpu
from jax.sharding import PartitionSpec as P

TILE = 128
REACH = 2
INLINE_GRAD = 2
MESH = pl.DeviceIdType.MESH


def sweep_kernel(
    ncol, nsec, pairs, src_ref, env_hbm, b_hbm, left_hbm, env_out, grad_out,
    b_v, a_v, left_v, land, win, fresh, grad_v, wide,
    recv_sem, send_sem, b_sem, left_sem, out_sem, gout_sem,
):
    col = lax.axis_index("col")
    sec = lax.axis_index("sec")
    tiles = left_v.shape[0] // TILE
    odd = sec % 2
    first = col == ncol - 1
    has_below = sec > 0
    has_above = sec < nsec - 1
    side = 2 * odd - 1
    has_pre = jnp.logical_and(sec + side >= 0, sec + side < nsec)
    has_post = jnp.logical_and(sec - side >= 0, sec - side < nsec)

    def local(p):
        return p + odd * (tiles - 1 - 2 * p)

    def slot(p):
        return local(p) + REACH

    def slot_beside(p):
        return tiles - 1 - p + odd * (2 * p + 1 - tiles) + REACH

    def rows(t):
        return pl.ds(pl.multiple_of(t * TILE, TILE), TILE)

    def mixed(t):
        return pl.ds(pl.multiple_of(t * pairs * TILE, pairs * TILE), pairs * TILE)

    def load_b(t):
        return pltpu.make_async_copy(b_hbm.at[mixed(t)], b_v.at[mixed(t)], b_sem.at[t])

    def load_left():
        return pltpu.make_async_copy(left_hbm, left_v, left_sem)

    def load_env(t):
        return pltpu.make_async_copy(env_hbm.at[rows(t)], land.at[t + REACH], recv_sem.at[t + REACH])

    def store_env(t):
        return pltpu.make_async_copy(fresh.at[rows(t)], env_out.at[rows(t)], out_sem.at[t])

    def store_grad(t):
        return pltpu.make_async_copy(grad_v.at[mixed(t)], grad_out.at[mixed(t)], gout_sem.at[t])

    def send(src, t, w, sem, to_col, to_sec):
        return pltpu.make_async_remote_copy(
            src_ref=src.at[rows(t)],
            dst_ref=land.at[w],
            send_sem=send_sem.at[sem],
            recv_sem=recv_sem.at[w],
            device_id=(to_col, to_sec),
            device_id_type=MESH,
        )

    def send_on(p):
        return send(fresh, local(p), slot(p), p, col - 1, sec)

    def send_pre(src, p, to_col, at):
        return send(src, local(p), slot_beside(-1 - p), tiles + at + p, to_col, sec + side)

    def send_post(src, p, to_col, at):
        return send(src, local(p), slot_beside(2 * tiles - 1 - p), tiles + at + p - tiles + 2 * REACH, to_col, sec - side)

    barrier = pltpu.get_barrier_semaphore()

    def greet(to_col, to_sec):
        pl.semaphore_signal(barrier, inc=1, device_id=(to_col, to_sec), device_id_type=MESH)

    @pl.when(jnp.logical_not(first))
    def _():
        greet(col + 1, sec)

    behind = jnp.minimum(col + 1, ncol - 1)

    @pl.when(has_below)
    def _():
        greet(behind, sec - 1)

    @pl.when(has_above)
    def _():
        greet(behind, sec + 1)

    def start_loads(p, carry):
        t = local(p)

        @pl.when(first)
        def _():
            load_env(t).start()

        load_b(t).start()
        return carry

    lax.fori_loop(0, tiles, start_loads, 0)
    load_left().start()

    def count(flag):
        return flag.astype(jnp.int32)

    beside = count(has_below) + count(has_above)

    @pl.when(col > 0)
    def _():
        pl.semaphore_wait(barrier, 1 + beside + count(first) * beside)

    def edges(do):
        @pl.when(jnp.logical_and(first, has_pre))
        def _():
            for u in range(REACH):
                do(send_pre(env_hbm, u, col, 2 * REACH))

        @pl.when(jnp.logical_and(first, has_post))
        def _():
            for u in range(REACH):
                do(send_post(env_hbm, tiles - REACH + u, col, 2 * REACH))

    edges(lambda copy: copy.start())
    win[...] = jnp.zeros_like(win)

    def sort_rows(t):
        load_b(t).wait()
        wide[...] = b_v[mixed(t), :].astype(jnp.float32)
        for j in range(pairs):
            part = wide[pl.ds(j, TILE, stride=pairs), :]
            a_v[rows(t), j * TILE:(j + 1) * TILE] = part.astype(jnp.bfloat16)

    @pl.when(jnp.logical_not(first))
    def _():
        def one(p, carry):
            sort_rows(local(p))
            return carry

        lax.fori_loop(0, tiles, one, 0)

    def take(p):
        w = slot(p)
        pltpu.make_async_copy(land.at[w], land.at[w], recv_sem.at[w]).wait()
        win[w] = land[w]

    @pl.when(has_pre)
    def _():
        for u in range(REACH):
            take(-1 - u)

    for u in range(REACH):
        take(u)

    def picked(t):
        parts = []
        for j in range(pairs):
            i = src_ref[j, t] - sec * tiles + REACH
            parts.append(win[jnp.clip(i, 0, win.shape[0] - 1)])
        return jnp.concatenate(parts, axis=0)

    def gradient(t):
        g = lax.dot_general(
            left_v[rows(t), :], picked(t), (((1,), (1,)), ((), ())), preferred_element_type=jnp.float32
        )
        for j in range(pairs):
            wide[pl.ds(j, TILE, stride=pairs), :] = g[:, j * TILE:(j + 1) * TILE]
        grad_v[mixed(t), :] = wide[...].astype(jnp.bfloat16)
        store_grad(t).start()

    load_left().wait()

    def step(p, carry):
        t = local(p)

        @pl.when(first)
        def _():
            sort_rows(t)

        @pl.when(jnp.logical_or(p + REACH < tiles, has_post))
        def _():
            take(p + REACH)

        acc = jnp.dot(a_v[rows(t), :], picked(t), preferred_element_type=jnp.float32)
        fresh[rows(t), :] = acc.astype(jnp.bfloat16)

        @pl.when(col > 0)
        def _():
            @pl.when(jnp.logical_and(p < REACH, has_pre))
            def _():
                send_pre(fresh, p, col - 1, 0).start()

            send_on(p).start()

            @pl.when(jnp.logical_and(p >= tiles - REACH, has_post))
            def _():
                send_post(fresh, p, col - 1, 0).start()

        store_env(t).start()

        @pl.when(col < INLINE_GRAD)
        def _():
            gradient(t)

        return carry

    lax.fori_loop(0, tiles, step, 0)

    @pl.when(col >= INLINE_GRAD)
    def _():
        def one(p, carry):
            gradient(local(p))
            return carry

        lax.fori_loop(0, tiles, one, 0)

    def drain(p, carry):
        store_env(local(p)).wait()
        store_grad(local(p)).wait()

        @pl.when(col > 0)
        def _():
            send_on(p).wait_send()

        return carry

    lax.fori_loop(0, tiles, drain, 0)

    @pl.when(jnp.logical_and(col > 0, has_pre))
    def _():
        for u in range(REACH):
            send_pre(fresh, u, col - 1, 0).wait_send()

    @pl.when(jnp.logical_and(col > 0, has_post))
    def _():
        for u in range(REACH):
            send_post(fresh, tiles - REACH + u, col - 1, 0).wait_send()

    edges(lambda copy: copy.wait_send())


def per_device(env_right, transfer, sources, env_left):
    ncol = lax.axis_size("col")
    nsec = lax.axis_size("sec")
    length = transfer.shape[2]
    pairs = transfer.shape[3]
    width = env_right.shape[2]
    tiles = length // TILE
    b = transfer.reshape(length * pairs, TILE)
    left = env_left.reshape(length, width)
    src = jnp.transpose(sources.reshape(tiles, pairs))
    bf16 = jnp.bfloat16
    in_hbm = pl.BlockSpec(memory_space=pltpu.HBM)
    anywhere = pl.BlockSpec(memory_space=pl.ANY)
    env, grad = pl.pallas_call(
        functools.partial(sweep_kernel, ncol, nsec, pairs),
        out_shape=(
            jax.ShapeDtypeStruct((length, width), bf16),
            jax.ShapeDtypeStruct((length * pairs, TILE), bf16),
        ),
        in_specs=[pl.BlockSpec(memory_space=pltpu.SMEM), in_hbm, in_hbm, in_hbm],
        out_specs=(anywhere, anywhere),
        scratch_shapes=[
            pltpu.VMEM((length * pairs, TILE), bf16),
            pltpu.VMEM((length, pairs * TILE), bf16),
            pltpu.VMEM((length, width), bf16),
            pltpu.VMEM((tiles + 2 * REACH, TILE, width), bf16),
            pltpu.VMEM((tiles + 2 * REACH, TILE, width), bf16),
            pltpu.VMEM((length, width), bf16),
            pltpu.VMEM((length * pairs, TILE), bf16),
            pltpu.VMEM((pairs * TILE, TILE), jnp.float32),
            pltpu.SemaphoreType.DMA((tiles + 2 * REACH,)),
            pltpu.SemaphoreType.DMA((tiles + 4 * REACH,)),
            pltpu.SemaphoreType.DMA((tiles,)),
            pltpu.SemaphoreType.DMA,
            pltpu.SemaphoreType.DMA((tiles,)),
            pltpu.SemaphoreType.DMA((tiles,)),
        ],
        compiler_params=pltpu.CompilerParams(
            collective_id=0, has_side_effects=True, vmem_limit_bytes=24 * 1024 * 1024
        ),
        name="sweep",
    )(src, *(pltpu.with_memory_space_constraint(x, pltpu.HBM) for x in (env_right.reshape(length, width), b, left)))
    return env.reshape(1, 1, length, width), grad.reshape(1, 1, length, pairs, TILE)


def solution(mesh):
    placed = (
        P(None, "sec", None),
        P("col", None, "sec", None, None),
        P("col", None, "sec", None),
        P("col", None, "sec", None),
    )
    return jax.shard_map(
        per_device,
        mesh=mesh,
        in_specs=placed,
        out_specs=(P("col", None, "sec", None), P("col", None, "sec", None, None)),
        check_vma=False,
    )
```

```python
import functools

import jax
import jax.numpy as jnp
from jax import lax
from jax.experimental import pallas as pl
from jax.experimental.pallas import tpu as pltpu
from jax.sharding import PartitionSpec as P

TILE = 128
REACH = 2
EDGE = 2 * REACH
GROUP = 4
MESH = pl.DeviceIdType.MESH


def sweep_kernel(
    ncol, nsec, pairs, src_ref, env_hbm, b_hbm, left_hbm, env_out, grad_out,
    b_v, a_v, left_v, env_v, land, win, fresh, grad_v, wide, spread, halo_a,
    recv_sem, send_sem, b_sem, left_sem, env_sem, out_sem, gout_sem, spread_sem, halo_sem,
):
    col = lax.axis_index("col")
    sec = lax.axis_index("sec")
    tiles = left_v.shape[0] // TILE
    groups = tiles // GROUP
    odd = sec % 2
    first = col == ncol - 1
    wider = jnp.logical_and(col % 2 == 1, jnp.logical_not(first))
    has_below = sec > 0
    has_above = sec < nsec - 1
    side = 2 * odd - 1
    has_pre = jnp.logical_and(sec + side >= 0, sec + side < nsec)
    has_post = jnp.logical_and(sec - side >= 0, sec - side < nsec)

    def local(p):
        return p + odd * (tiles - 1 - 2 * p)

    def slot(p):
        return local(p) + EDGE

    def slot_beside(p):
        return tiles - 1 - p + odd * (2 * p + 1 - tiles) + EDGE

    def rows(t):
        return pl.ds(pl.multiple_of(t * TILE, TILE), TILE)

    def mixed(t, n=1):
        return pl.ds(pl.multiple_of(t * pairs * TILE, pairs * TILE), n * pairs * TILE)

    def load_b(g):
        span = mixed(g * GROUP, GROUP)
        return pltpu.make_async_copy(b_hbm.at[span], b_v.at[span], b_sem.at[g])

    load_left = pltpu.make_async_copy(left_hbm, left_v, left_sem)
    load_env = pltpu.make_async_copy(env_hbm, env_v, env_sem)
    store_env = pltpu.make_async_copy(fresh.at[pl.ds(REACH, tiles)], env_out, out_sem)

    def store_grad(i):
        span = mixed(2 * i, 2)
        return pltpu.make_async_copy(grad_v.at[span], grad_out.at[span], gout_sem.at[i])

    def send(src, w, sem, to_col, to_sec):
        return pltpu.make_async_remote_copy(
            src_ref=src,
            dst_ref=land.at[w],
            send_sem=send_sem.at[sem],
            recv_sem=recv_sem.at[w],
            device_id=(to_col, to_sec),
            device_id_type=MESH,
        )

    def held(p):
        return fresh.at[local(p) + REACH]

    def send_on(p):
        return send(held(p), slot(p), p + REACH, col - 1, sec)

    after = tiles + 2 * REACH

    def send_pre(src, p, to_col, at):
        return send(src, slot_beside(-1 - p), after + at + p, to_col, sec + side)

    def send_post(src, p, to_col, at):
        return send(src, slot_beside(2 * tiles - 1 - p), after + at + EDGE + tiles - 1 - p, to_col, sec - side)

    def send_spread(h, to_sec):
        return pltpu.make_async_remote_copy(
            src_ref=spread.at[h],
            dst_ref=halo_a.at[h],
            send_sem=spread_sem.at[h],
            recv_sem=halo_sem.at[h],
            device_id=(col, to_sec),
            device_id_type=MESH,
        )

    barrier = pltpu.get_barrier_semaphore()

    def greet(to_col, to_sec):
        pl.semaphore_signal(barrier, inc=1, device_id=(to_col, to_sec), device_id_type=MESH)

    @pl.when(jnp.logical_not(first))
    def _():
        greet(col + 1, sec)

    behind = jnp.minimum(col + 1, ncol - 1)
    meets = jnp.logical_or(col % 2 == 1, col == ncol - 2)
    for there, by in ((has_below, -1), (has_above, 1)):
        @pl.when(jnp.logical_and(there, meets))
        def _():
            greet(behind, sec + by)

        @pl.when(jnp.logical_and(there, wider))
        def _():
            greet(col, sec + by)

    @pl.when(first)
    def _():
        load_env.start()

    def start_loads(i, carry):
        load_b(i + odd * (groups - 1 - 2 * i)).start()
        return carry

    lax.fori_loop(0, groups, start_loads, 0)
    load_left.start()

    def count(flag):
        return flag.astype(jnp.int32)

    beside = count(has_below) + count(has_above)

    @pl.when(col > 0)
    def _():
        pl.semaphore_wait(barrier, 1 + beside + count(first) * beside)

    def first_edges(do):
        @pl.when(jnp.logical_and(first, has_pre))
        def _():
            for u in range(REACH):
                do(send_pre(env_hbm.at[rows(local(u))], u, col, 2 * EDGE))

        @pl.when(jnp.logical_and(first, has_post))
        def _():
            for u in range(REACH):
                p = tiles - 1 - u
                do(send_post(env_hbm.at[rows(local(p))], p, col, 2 * EDGE))

    first_edges(lambda copy: copy.start())
    win[...] = jnp.zeros_like(win)

    def sort_rows(t):
        wide[0] = b_v[mixed(t), :].astype(jnp.float32)
        for j in range(pairs):
            part = wide[0, pl.ds(j, TILE, stride=pairs), :]
            a_v[rows(t), j * TILE:(j + 1) * TILE] = part.astype(jnp.bfloat16)

    def sort_group(i):
        g = i + odd * (groups - 1 - 2 * i)
        load_b(g).wait()
        for u in range(GROUP):
            sort_rows(g * GROUP + u)

    def by_offset(t, h):
        blocks = [a_v[rows(t), j * TILE:(j + 1) * TILE].astype(jnp.float32) for j in range(pairs)]
        for k in range(2 * REACH + 1):
            total = jnp.zeros((TILE, TILE), jnp.float32)
            for j in range(pairs):
                here = src_ref[j, t] - sec * tiles - t == k - REACH
                total = total + jnp.where(here, blocks[j], 0.0)
            spread[h, :, k * TILE:(k + 1) * TILE] = total.astype(jnp.bfloat16)

    def edge_spreads(do):
        @pl.when(jnp.logical_and(wider, has_pre))
        def _():
            for u in range(REACH):
                do(u, send_spread(u, sec + side))

        @pl.when(jnp.logical_and(wider, has_post))
        def _():
            for u in range(REACH):
                do(tiles - 1 - u, send_spread(REACH + u, sec - side))

    @pl.when(jnp.logical_not(first))
    def _():
        sort_group(0)
        sort_group(groups - 1)

        @pl.when(wider)
        def _():
            for u in range(REACH):
                by_offset(local(u), u)
                by_offset(local(tiles - 1 - u), REACH + u)

        edge_spreads(lambda p, copy: copy.start())

        def one(i, carry):
            sort_group(i)
            return carry

        lax.fori_loop(1, groups - 1, one, 0)

    load_left.wait()

    def arrive(p):
        w = slot(p)
        pltpu.make_async_copy(land.at[w], land.at[w], recv_sem.at[w]).wait()
        win[w] = land[w]

    def take(p):
        @pl.when(first)
        def _():
            win[slot(p)] = env_v[rows(local(p)), :]

        @pl.when(jnp.logical_not(first))
        def _():
            arrive(p)

    @pl.when(first)
    def _():
        load_env.wait()

    def picked(t):
        parts = []
        for j in range(pairs):
            i = src_ref[j, t] - sec * tiles + EDGE
            parts.append(win[jnp.clip(i, 0, win.shape[0] - 1)])
        return jnp.concatenate(parts, axis=0)

    def halo_tiles(ps, hs):
        for p, h in zip(ps, hs):
            w = slot(p)
            near = win[pl.ds(w - REACH, 2 * REACH + 1)].reshape((2 * REACH + 1) * TILE, TILE)
            acc = jnp.dot(halo_a[h], near, preferred_element_type=jnp.float32)
            fresh[local(p) + REACH] = acc.astype(jnp.bfloat16)
        for p in ps:
            send_on(p).start()

    def gradient(t, u):
        g = lax.dot_general(
            left_v[rows(t), :], picked(t), (((1,), (1,)), ((), ())), preferred_element_type=jnp.float32
        )
        for j in range(pairs):
            wide[u, pl.ds(j, TILE, stride=pairs), :] = g[:, j * TILE:(j + 1) * TILE]
        grad_v[mixed(t), :] = wide[u].astype(jnp.bfloat16)

    @pl.when(has_pre)
    def _():
        for u in range(REACH):
            arrive(-1 - u)

        @pl.when(wider)
        def _():
            for u in range(REACH, EDGE):
                arrive(-1 - u)

    for u in range(REACH):
        take(u)

    def halo_ready(hs):
        for h in hs:
            pltpu.make_async_copy(halo_a.at[h], halo_a.at[h], halo_sem.at[h]).wait()

    @pl.when(jnp.logical_and(wider, has_pre))
    def _():
        halo_ready((0, 1))
        halo_tiles((-2, -1), (1, 0))

    sends_edges = jnp.logical_and(col > 0, jnp.logical_not(wider))
    out_reach = jnp.where(first, REACH, EDGE)

    def step(p, carry):
        t = local(p)

        @pl.when(jnp.logical_and(first, p % GROUP == 0))
        def _():
            sort_group(p // GROUP)

        @pl.when(p + REACH < tiles)
        def _():
            take(p + REACH)

        @pl.when(jnp.logical_and(p + REACH >= tiles, has_post))
        def _():
            arrive(p + REACH)

        acc = jnp.dot(a_v[rows(t), :], picked(t), preferred_element_type=jnp.float32)
        fresh[t + REACH] = acc.astype(jnp.bfloat16)

        @pl.when(col > 0)
        def _():
            @pl.when(jnp.logical_and(jnp.logical_and(p < out_reach, has_pre), sends_edges))
            def _():
                send_pre(held(p), p, col - 1, 0).start()

            send_on(p).start()

            @pl.when(jnp.logical_and(jnp.logical_and(p >= tiles - out_reach, has_post), sends_edges))
            def _():
                send_post(held(p), p, col - 1, 0).start()

        @pl.when(jnp.logical_and(col == 0, t % 2 == 1))
        def _():
            gradient(t, 0)

        return carry

    lax.fori_loop(0, tiles, step, 0)

    @pl.when(jnp.logical_and(wider, has_post))
    def _():
        arrive(tiles + REACH)
        arrive(tiles + REACH + 1)
        halo_ready((2, 3))
        halo_tiles((tiles, tiles + 1), (2, 3))

    store_env.start()

    @pl.when(col > 0)
    def _():
        def two(i, carry):
            gradient(2 * i, 0)
            gradient(2 * i + 1, 1)
            store_grad(i).start()
            return carry

        lax.fori_loop(0, tiles // 2, two, 0)

    @pl.when(col == 0)
    def _():
        def two(i, carry):
            gradient(4 * i, 0)
            gradient(4 * i + 2, 1)
            store_grad(2 * i).start()
            store_grad(2 * i + 1).start()
            return carry

        lax.fori_loop(0, tiles // 4, two, 0)

    @pl.when(col > 0)
    def _():
        def sent(p, carry):
            send_on(p).wait_send()
            return carry

        lax.fori_loop(0, tiles, sent, 0)

    for there, at in ((has_pre, -REACH), (has_post, tiles)):
        @pl.when(jnp.logical_and(wider, there))
        def _():
            for u in range(REACH):
                send_on(at + u).wait_send()

    edge_spreads(lambda p, copy: copy.wait_send())

    for u in range(EDGE):
        sent_edge = jnp.logical_and(sends_edges, u < out_reach)

        @pl.when(jnp.logical_and(sent_edge, has_pre))
        def _():
            send_pre(held(u), u, col - 1, 0).wait_send()

        @pl.when(jnp.logical_and(sent_edge, has_post))
        def _():
            send_post(held(tiles - 1 - u), tiles - 1 - u, col - 1, 0).wait_send()

    first_edges(lambda copy: copy.wait_send())
    store_env.wait()

    def stored(i, carry):
        store_grad(i).wait()
        return carry

    lax.fori_loop(0, tiles // 2, stored, 0)


def per_device(env_right, transfer, sources, env_left):
    ncol = lax.axis_size("col")
    nsec = lax.axis_size("sec")
    length = transfer.shape[2]
    pairs = transfer.shape[3]
    width = env_right.shape[2]
    tiles = length // TILE
    b = transfer.reshape(length * pairs, TILE)
    left = env_left.reshape(length, width)
    src = jnp.transpose(sources.reshape(tiles, pairs))
    bf16 = jnp.bfloat16
    in_hbm = pl.BlockSpec(memory_space=pltpu.HBM)
    anywhere = pl.BlockSpec(memory_space=pl.ANY)
    dma = pltpu.SemaphoreType.DMA
    env, grad = pl.pallas_call(
        functools.partial(sweep_kernel, ncol, nsec, pairs),
        out_shape=(
            jax.ShapeDtypeStruct((tiles, TILE, width), bf16),
            jax.ShapeDtypeStruct((length * pairs, TILE), bf16),
        ),
        in_specs=[pl.BlockSpec(memory_space=pltpu.SMEM), in_hbm, in_hbm, in_hbm],
        out_specs=(anywhere, anywhere),
        scratch_shapes=[
            pltpu.VMEM((length * pairs, TILE), bf16),
            pltpu.VMEM((length, pairs * TILE), bf16),
            pltpu.VMEM((length, width), bf16),
            pltpu.VMEM((length, width), bf16),
            pltpu.VMEM((tiles + 2 * EDGE, TILE, width), bf16),
            pltpu.VMEM((tiles + 2 * EDGE, TILE, width), bf16),
            pltpu.VMEM((tiles + 2 * REACH, TILE, width), bf16),
            pltpu.VMEM((length * pairs, TILE), bf16),
            pltpu.VMEM((2, pairs * TILE, TILE), jnp.float32),
            pltpu.VMEM((2 * REACH, TILE, (2 * REACH + 1) * TILE), bf16),
            pltpu.VMEM((2 * REACH, TILE, (2 * REACH + 1) * TILE), bf16),
            dma((tiles + 2 * EDGE,)),
            dma((tiles + 2 * REACH + 4 * EDGE,)),
            dma((tiles // GROUP,)),
            dma,
            dma,
            dma,
            dma((tiles // 2,)),
            dma((2 * REACH,)),
            dma((2 * REACH,)),
        ],
        compiler_params=pltpu.CompilerParams(
            collective_id=0, has_side_effects=True, vmem_limit_bytes=24 * 1024 * 1024
        ),
        name="sweep",
    )(src, *(pltpu.with_memory_space_constraint(x, pltpu.HBM) for x in (env_right.reshape(length, width), b, left)))
    return env.reshape(1, 1, length, width), grad.reshape(1, 1, length, pairs, TILE)


def solution(mesh):
    placed = (
        P(None, "sec", None),
        P("col", None, "sec", None, None),
        P("col", None, "sec", None),
        P("col", None, "sec", None),
    )
    return jax.shard_map(
        per_device,
        mesh=mesh,
        in_specs=placed,
        out_specs=(P("col", None, "sec", None), P("col", None, "sec", None, None)),
        check_vma=False,
    )
```

```python
import functools

import jax
import jax.numpy as jnp
from jax import lax
from jax.experimental import pallas as pl
from jax.experimental.pallas import tpu as pltpu
from jax.sharding import PartitionSpec as P

TILE = 128
REACH = 2
EDGE = 2 * REACH
GROUP = 4
MESH = pl.DeviceIdType.MESH


def sweep_kernel(
    ncol, nsec, pairs, src_ref, env_hbm, b_hbm, left_hbm, env_out, grad_out,
    b_v, a_v, left_v, env_v, land, win, fresh, grad_v, wide, spread, halo_a,
    recv_sem, send_sem, b_sem, left_sem, env_sem, out_sem, gout_sem, spread_sem, halo_sem,
):
    col = lax.axis_index("col")
    sec = lax.axis_index("sec")
    tiles = left_v.shape[0] // TILE
    groups = tiles // GROUP
    odd = 1 - sec % 2
    first = col == ncol - 1
    wider = jnp.logical_and(col % 2 == 1, jnp.logical_not(first))
    has_below = sec > 0
    has_above = sec < nsec - 1
    side = 2 * odd - 1
    has_pre = jnp.logical_and(sec + side >= 0, sec + side < nsec)
    has_post = jnp.logical_and(sec - side >= 0, sec - side < nsec)

    def local(p):
        return p + odd * (tiles - 1 - 2 * p)

    def slot(p):
        return local(p) + EDGE

    def slot_beside(p):
        return tiles - 1 - p + odd * (2 * p + 1 - tiles) + EDGE

    def rows(t):
        return pl.ds(pl.multiple_of(t * TILE, TILE), TILE)

    def mixed(t, n=1):
        return pl.ds(pl.multiple_of(t * pairs * TILE, pairs * TILE), n * pairs * TILE)

    def load_b(g):
        span = mixed(g * GROUP, GROUP)
        return pltpu.make_async_copy(b_hbm.at[span], b_v.at[span], b_sem.at[g])

    load_left = pltpu.make_async_copy(left_hbm, left_v, left_sem)
    load_env = pltpu.make_async_copy(env_hbm, env_v, env_sem)
    store_env = pltpu.make_async_copy(fresh.at[pl.ds(REACH, tiles)], env_out, out_sem)

    def store_grad(i):
        span = mixed(2 * i, 2)
        return pltpu.make_async_copy(grad_v.at[span], grad_out.at[span], gout_sem.at[i])

    def send(src, w, sem, to_col, to_sec):
        return pltpu.make_async_remote_copy(
            src_ref=src,
            dst_ref=land.at[w],
            send_sem=send_sem.at[sem],
            recv_sem=recv_sem.at[w],
            device_id=(to_col, to_sec),
            device_id_type=MESH,
        )

    def held(p):
        return fresh.at[local(p) + REACH]

    def send_on(p):
        return send(held(p), slot(p), p + REACH, col - 1, sec)

    after = tiles + 2 * REACH

    def send_pre(src, p, to_col, at):
        return send(src, slot_beside(-1 - p), after + at + p, to_col, sec + side)

    def send_post(src, p, to_col, at):
        return send(src, slot_beside(2 * tiles - 1 - p), after + at + EDGE + tiles - 1 - p, to_col, sec - side)

    def send_spread(h, to_sec):
        return pltpu.make_async_remote_copy(
            src_ref=spread.at[h],
            dst_ref=halo_a.at[h],
            send_sem=spread_sem.at[h],
            recv_sem=halo_sem.at[h],
            device_id=(col, to_sec),
            device_id_type=MESH,
        )

    barrier = pltpu.get_barrier_semaphore()

    def greet(to_col, to_sec):
        pl.semaphore_signal(barrier, inc=1, device_id=(to_col, to_sec), device_id_type=MESH)

    @pl.when(jnp.logical_not(first))
    def _():
        greet(col + 1, sec)

    behind = jnp.minimum(col + 1, ncol - 1)
    meets = jnp.logical_or(col % 2 == 1, col == ncol - 2)
    for there, by in ((has_below, -1), (has_above, 1)):
        @pl.when(jnp.logical_and(there, meets))
        def _():
            greet(behind, sec + by)

        @pl.when(jnp.logical_and(there, wider))
        def _():
            greet(col, sec + by)

    @pl.when(first)
    def _():
        load_env.start()

    def start_loads(i, carry):
        load_b(i + odd * (groups - 1 - 2 * i)).start()
        return carry

    lax.fori_loop(0, groups, start_loads, 0)
    load_left.start()

    def count(flag):
        return flag.astype(jnp.int32)

    beside = count(has_below) + count(has_above)

    @pl.when(col > 0)
    def _():
        pl.semaphore_wait(barrier, 1 + beside + count(first) * beside)

    def first_edges(do):
        @pl.when(jnp.logical_and(first, has_pre))
        def _():
            for u in range(REACH):
                do(send_pre(env_hbm.at[rows(local(u))], u, col, 2 * EDGE))

        @pl.when(jnp.logical_and(first, has_post))
        def _():
            for u in range(REACH):
                p = tiles - 1 - u
                do(send_post(env_hbm.at[rows(local(p))], p, col, 2 * EDGE))

    first_edges(lambda copy: copy.start())
    win[...] = jnp.zeros_like(win)

    def sort_rows(t):
        wide[0] = b_v[mixed(t), :].astype(jnp.float32)
        for j in range(pairs):
            part = wide[0, pl.ds(j, TILE, stride=pairs), :]
            a_v[rows(t), j * TILE:(j + 1) * TILE] = part.astype(jnp.bfloat16)

    def sort_group(i):
        g = i + odd * (groups - 1 - 2 * i)
        load_b(g).wait()
        for u in range(GROUP):
            sort_rows(g * GROUP + u)

    def by_offset(t, h):
        blocks = [a_v[rows(t), j * TILE:(j + 1) * TILE].astype(jnp.float32) for j in range(pairs)]
        for k in range(2 * REACH + 1):
            total = jnp.zeros((TILE, TILE), jnp.float32)
            for j in range(pairs):
                here = src_ref[j, t] - sec * tiles - t == k - REACH
                total = total + jnp.where(here, blocks[j], 0.0)
            spread[h, :, k * TILE:(k + 1) * TILE] = total.astype(jnp.bfloat16)

    def edge_spreads(do):
        @pl.when(jnp.logical_and(wider, has_pre))
        def _():
            for u in range(REACH):
                do(u, send_spread(u, sec + side))

        @pl.when(jnp.logical_and(wider, has_post))
        def _():
            for u in range(REACH):
                do(tiles - 1 - u, send_spread(REACH + u, sec - side))

    @pl.when(jnp.logical_not(first))
    def _():
        sort_group(0)
        sort_group(groups - 1)

        @pl.when(wider)
        def _():
            for u in range(REACH):
                by_offset(local(u), u)
                by_offset(local(tiles - 1 - u), REACH + u)

        edge_spreads(lambda p, copy: copy.start())

        def one(i, carry):
            sort_group(i)
            return carry

        lax.fori_loop(1, groups - 1, one, 0)

    load_left.wait()

    def arrive(p):
        w = slot(p)
        pltpu.make_async_copy(land.at[w], land.at[w], recv_sem.at[w]).wait()
        win[w] = land[w]

    def take(p):
        @pl.when(first)
        def _():
            win[slot(p)] = env_v[rows(local(p)), :]

        @pl.when(jnp.logical_not(first))
        def _():
            arrive(p)

    @pl.when(first)
    def _():
        load_env.wait()

    def picked(t):
        parts = []
        for j in range(pairs):
            i = src_ref[j, t] - sec * tiles + EDGE
            parts.append(win[jnp.clip(i, 0, win.shape[0] - 1)])
        return jnp.concatenate(parts, axis=0)

    def halo_tiles(ps, hs):
        for p, h in zip(ps, hs):
            w = slot(p)
            near = win[pl.ds(w - REACH, 2 * REACH + 1)].reshape((2 * REACH + 1) * TILE, TILE)
            acc = jnp.dot(halo_a[h], near, preferred_element_type=jnp.float32)
            fresh[local(p) + REACH] = acc.astype(jnp.bfloat16)

    def gradient(t, u):
        g = lax.dot_general(
            left_v[rows(t), :], picked(t), (((1,), (1,)), ((), ())), preferred_element_type=jnp.float32
        )
        for j in range(pairs):
            wide[u, pl.ds(j, TILE, stride=pairs), :] = g[:, j * TILE:(j + 1) * TILE]
        grad_v[mixed(t), :] = wide[u].astype(jnp.bfloat16)

    @pl.when(has_pre)
    def _():
        for u in range(REACH):
            arrive(-1 - u)

        @pl.when(wider)
        def _():
            for u in range(REACH, EDGE):
                arrive(-1 - u)

    for u in range(REACH):
        take(u)

    def halo_ready(hs):
        for h in hs:
            pltpu.make_async_copy(halo_a.at[h], halo_a.at[h], halo_sem.at[h]).wait()

    sends_edges = jnp.logical_and(col > 0, jnp.logical_not(wider))
    out_reach = jnp.where(first, REACH, EDGE)

    def own_tile(t):
        acc = jnp.dot(a_v[rows(t), :], picked(t), preferred_element_type=jnp.float32)
        fresh[t + REACH] = acc.astype(jnp.bfloat16)

    def pass_on(p):
        @pl.when(jnp.logical_and(jnp.logical_and(p < out_reach, has_pre), sends_edges))
        def _():
            send_pre(held(p), p, col - 1, 0).start()

        @pl.when(col > 0)
        def _():
            send_on(p).start()

        @pl.when(jnp.logical_and(jnp.logical_and(p >= tiles - out_reach, has_post), sends_edges))
        def _():
            send_post(held(p), p, col - 1, 0).start()

    early = jnp.logical_and(wider, has_pre)

    @pl.when(early)
    def _():
        take(REACH)
        halo_ready((0, 1))
        halo_tiles((-2, -1), (1, 0))
        own_tile(local(0))
        for p in (-2, -1, 0):
            send_on(p).start()

    def step(p, carry):
        t = local(p)

        @pl.when(jnp.logical_and(first, p % GROUP == 0))
        def _():
            sort_group(p // GROUP)

        @pl.when(p + REACH < tiles)
        def _():
            take(p + REACH)

        @pl.when(jnp.logical_and(p + REACH >= tiles, has_post))
        def _():
            arrive(p + REACH)

        own_tile(t)
        pass_on(p)

        @pl.when(jnp.logical_and(col == 0, t % 2 == 1))
        def _():
            gradient(t, 0)

        return carry

    lax.fori_loop(count(early), tiles, step, 0)

    @pl.when(jnp.logical_and(wider, has_post))
    def _():
        arrive(tiles + REACH)
        arrive(tiles + REACH + 1)
        halo_ready((2, 3))
        halo_tiles((tiles, tiles + 1), (2, 3))
        for p in (tiles, tiles + 1):
            send_on(p).start()

    store_env.start()

    @pl.when(col > 0)
    def _():
        def two(i, carry):
            gradient(2 * i, 0)
            gradient(2 * i + 1, 1)
            store_grad(i).start()
            return carry

        lax.fori_loop(0, tiles // 2, two, 0)

    @pl.when(col == 0)
    def _():
        def two(i, carry):
            gradient(4 * i, 0)
            gradient(4 * i + 2, 1)
            store_grad(2 * i).start()
            store_grad(2 * i + 1).start()
            return carry

        lax.fori_loop(0, tiles // 4, two, 0)

    @pl.when(col > 0)
    def _():
        def sent(p, carry):
            send_on(p).wait_send()
            return carry

        lax.fori_loop(0, tiles, sent, 0)

    for there, at in ((has_pre, -REACH), (has_post, tiles)):
        @pl.when(jnp.logical_and(wider, there))
        def _():
            for u in range(REACH):
                send_on(at + u).wait_send()

    edge_spreads(lambda p, copy: copy.wait_send())

    for u in range(EDGE):
        sent_edge = jnp.logical_and(sends_edges, u < out_reach)

        @pl.when(jnp.logical_and(sent_edge, has_pre))
        def _():
            send_pre(held(u), u, col - 1, 0).wait_send()

        @pl.when(jnp.logical_and(sent_edge, has_post))
        def _():
            send_post(held(tiles - 1 - u), tiles - 1 - u, col - 1, 0).wait_send()

    first_edges(lambda copy: copy.wait_send())
    store_env.wait()

    def stored(i, carry):
        store_grad(i).wait()
        return carry

    lax.fori_loop(0, tiles // 2, stored, 0)


def per_device(env_right, transfer, sources, env_left):
    ncol = lax.axis_size("col")
    nsec = lax.axis_size("sec")
    length = transfer.shape[2]
    pairs = transfer.shape[3]
    width = env_right.shape[2]
    tiles = length // TILE
    b = transfer.reshape(length * pairs, TILE)
    left = env_left.reshape(length, width)
    src = jnp.transpose(sources.reshape(tiles, pairs))
    bf16 = jnp.bfloat16
    in_hbm = pl.BlockSpec(memory_space=pltpu.HBM)
    anywhere = pl.BlockSpec(memory_space=pl.ANY)
    dma = pltpu.SemaphoreType.DMA
    env, grad = pl.pallas_call(
        functools.partial(sweep_kernel, ncol, nsec, pairs),
        out_shape=(
            jax.ShapeDtypeStruct((tiles, TILE, width), bf16),
            jax.ShapeDtypeStruct((length * pairs, TILE), bf16),
        ),
        in_specs=[pl.BlockSpec(memory_space=pltpu.SMEM), in_hbm, in_hbm, in_hbm],
        out_specs=(anywhere, anywhere),
        scratch_shapes=[
            pltpu.VMEM((length * pairs, TILE), bf16),
            pltpu.VMEM((length, pairs * TILE), bf16),
            pltpu.VMEM((length, width), bf16),
            pltpu.VMEM((length, width), bf16),
            pltpu.VMEM((tiles + 2 * EDGE, TILE, width), bf16),
            pltpu.VMEM((tiles + 2 * EDGE, TILE, width), bf16),
            pltpu.VMEM((tiles + 2 * REACH, TILE, width), bf16),
            pltpu.VMEM((length * pairs, TILE), bf16),
            pltpu.VMEM((2, pairs * TILE, TILE), jnp.float32),
            pltpu.VMEM((2 * REACH, TILE, (2 * REACH + 1) * TILE), bf16),
            pltpu.VMEM((2 * REACH, TILE, (2 * REACH + 1) * TILE), bf16),
            dma((tiles + 2 * EDGE,)),
            dma((tiles + 2 * REACH + 4 * EDGE,)),
            dma((tiles // GROUP,)),
            dma,
            dma,
            dma,
            dma((tiles // 2,)),
            dma((2 * REACH,)),
            dma((2 * REACH,)),
        ],
        compiler_params=pltpu.CompilerParams(
            collective_id=0, has_side_effects=True, vmem_limit_bytes=24 * 1024 * 1024
        ),
        name="sweep",
    )(src, *(pltpu.with_memory_space_constraint(x, pltpu.HBM) for x in (env_right.reshape(length, width), b, left)))
    return env.reshape(1, 1, length, width), grad.reshape(1, 1, length, pairs, TILE)


def solution(mesh):
    placed = (
        P(None, "sec", None),
        P("col", None, "sec", None, None),
        P("col", None, "sec", None),
        P("col", None, "sec", None),
    )
    return jax.shard_map(
        per_device,
        mesh=mesh,
        in_specs=placed,
        out_specs=(P("col", None, "sec", None), P("col", None, "sec", None, None)),
        check_vma=False,
    )
```

```python
import functools

import jax
import jax.numpy as jnp
from jax import lax
from jax.experimental import pallas as pl
from jax.experimental.pallas import tpu as pltpu
from jax.sharding import PartitionSpec as P

TILE = 128
REACH = 2
EDGE = 2 * REACH
GROUP = 4
MESH = pl.DeviceIdType.MESH


def sweep_kernel(
    ncol, nsec, pairs, src_ref, env_hbm, b_hbm, left_hbm, env_out, grad_out,
    b_v, a_v, left_v, env_v, land, win, fresh, grad_v, wide, spread, halo_a,
    recv_sem, send_sem, b_sem, left_sem, env_sem, out_sem, gout_sem, spread_sem, halo_sem,
):
    col = lax.axis_index("col")
    sec = lax.axis_index("sec")
    tiles = left_v.shape[0] // TILE
    groups = tiles // GROUP
    odd = 1 - sec % 2
    first = col == ncol - 1
    wider = jnp.logical_and(col % 2 == 1, jnp.logical_not(first))
    has_below = sec > 0
    has_above = sec < nsec - 1
    side = 2 * odd - 1
    has_pre = jnp.logical_and(sec + side >= 0, sec + side < nsec)
    has_post = jnp.logical_and(sec - side >= 0, sec - side < nsec)

    def local(p):
        return p + odd * (tiles - 1 - 2 * p)

    def slot(p):
        return local(p) + EDGE

    def slot_beside(p):
        return tiles - 1 - p + odd * (2 * p + 1 - tiles) + EDGE

    def rows(t):
        return pl.ds(pl.multiple_of(t * TILE, TILE), TILE)

    def mixed(t, n=1):
        return pl.ds(pl.multiple_of(t * pairs * TILE, pairs * TILE), n * pairs * TILE)

    def load_b(g):
        span = mixed(g * GROUP, GROUP)
        return pltpu.make_async_copy(b_hbm.at[span], b_v.at[span], b_sem.at[g])

    load_left = pltpu.make_async_copy(left_hbm, left_v, left_sem)
    load_env = pltpu.make_async_copy(env_hbm, env_v, env_sem)
    store_env = pltpu.make_async_copy(fresh.at[pl.ds(REACH, tiles)], env_out, out_sem)

    def store_grad(i):
        span = mixed(4 * i, 4)
        return pltpu.make_async_copy(grad_v.at[span], grad_out.at[span], gout_sem.at[i])

    def send(src, w, sem, to_col, to_sec):
        return pltpu.make_async_remote_copy(
            src_ref=src,
            dst_ref=land.at[w],
            send_sem=send_sem.at[sem],
            recv_sem=recv_sem.at[w],
            device_id=(to_col, to_sec),
            device_id_type=MESH,
        )

    def held(p):
        return fresh.at[local(p) + REACH]

    def send_on(p, own=None):
        return send(held(p), slot(p), REACH if own is None else own, col - 1, sec)

    after = 2 * REACH + 1

    def send_pre(src, p, to_col, at):
        return send(src, slot_beside(-1 - p), after + at + p, to_col, sec + side)

    def send_post(src, p, to_col, at):
        return send(src, slot_beside(2 * tiles - 1 - p), after + at + EDGE + tiles - 1 - p, to_col, sec - side)

    def send_spread(h, to_sec):
        return pltpu.make_async_remote_copy(
            src_ref=spread.at[h],
            dst_ref=halo_a.at[h],
            send_sem=spread_sem.at[h],
            recv_sem=halo_sem.at[h],
            device_id=(col, to_sec),
            device_id_type=MESH,
        )

    barrier = pltpu.get_barrier_semaphore()

    def greet(to_col, to_sec):
        pl.semaphore_signal(barrier, inc=1, device_id=(to_col, to_sec), device_id_type=MESH)

    @pl.when(jnp.logical_not(first))
    def _():
        greet(col + 1, sec)

    behind = jnp.minimum(col + 1, ncol - 1)
    meets = jnp.logical_or(col % 2 == 1, col == ncol - 2)
    for there, by in ((has_below, -1), (has_above, 1)):
        @pl.when(jnp.logical_and(there, meets))
        def _():
            greet(behind, sec + by)

        @pl.when(jnp.logical_and(there, wider))
        def _():
            greet(col, sec + by)

    @pl.when(first)
    def _():
        load_env.start()

    def start_loads(i, carry):
        load_b(i + odd * (groups - 1 - 2 * i)).start()
        return carry

    lax.fori_loop(0, groups, start_loads, 0)
    load_left.start()

    def count(flag):
        return flag.astype(jnp.int32)

    beside = count(has_below) + count(has_above)

    @pl.when(col > 0)
    def _():
        pl.semaphore_wait(barrier, 1 + beside + count(first) * beside)

    def first_edges(do):
        @pl.when(jnp.logical_and(first, has_pre))
        def _():
            for u in range(REACH):
                do(send_pre(env_hbm.at[rows(local(u))], u, col, 2 * EDGE))

        @pl.when(jnp.logical_and(first, has_post))
        def _():
            for u in range(REACH):
                p = tiles - 1 - u
                do(send_post(env_hbm.at[rows(local(p))], p, col, 2 * EDGE))

    first_edges(lambda copy: copy.start())
    win[...] = jnp.zeros_like(win)

    def sort_rows(t):
        wide[0] = b_v[mixed(t), :].astype(jnp.float32)
        for j in range(pairs):
            part = wide[0, pl.ds(j, TILE, stride=pairs), :]
            a_v[rows(t), j * TILE:(j + 1) * TILE] = part.astype(jnp.bfloat16)

    def sort_group(i):
        g = i + odd * (groups - 1 - 2 * i)
        load_b(g).wait()
        for u in range(GROUP):
            sort_rows(g * GROUP + u)

    def by_offset(t, h):
        blocks = [a_v[rows(t), j * TILE:(j + 1) * TILE].astype(jnp.float32) for j in range(pairs)]
        for k in range(2 * REACH + 1):
            total = jnp.zeros((TILE, TILE), jnp.float32)
            for j in range(pairs):
                here = src_ref[j, t] - sec * tiles - t == k - REACH
                total = total + jnp.where(here, blocks[j], 0.0)
            spread[h, :, k * TILE:(k + 1) * TILE] = total.astype(jnp.bfloat16)

    def edge_spreads(do):
        @pl.when(jnp.logical_and(wider, has_pre))
        def _():
            for u in range(REACH):
                do(u, send_spread(u, sec + side))

        @pl.when(jnp.logical_and(wider, has_post))
        def _():
            for u in range(REACH):
                do(tiles - 1 - u, send_spread(REACH + u, sec - side))

    @pl.when(jnp.logical_not(first))
    def _():
        sort_group(0)
        sort_group(groups - 1)

        @pl.when(wider)
        def _():
            for u in range(REACH):
                by_offset(local(u), u)
                by_offset(local(tiles - 1 - u), REACH + u)

        edge_spreads(lambda p, copy: copy.start())

        def one(i, carry):
            sort_group(i)
            return carry

        lax.fori_loop(1, groups - 1, one, 0)

    load_left.wait()

    def arrive(p):
        w = slot(p)
        pltpu.make_async_copy(land.at[w], land.at[w], recv_sem.at[w]).wait()
        win[w] = land[w]

    def take(p):
        @pl.when(first)
        def _():
            win[slot(p)] = env_v[rows(local(p)), :]

        @pl.when(jnp.logical_not(first))
        def _():
            arrive(p)

    @pl.when(first)
    def _():
        load_env.wait()

    def picked(t):
        parts = []
        for j in range(pairs):
            i = src_ref[j, t] - sec * tiles + EDGE
            parts.append(win[jnp.clip(i, 0, win.shape[0] - 1)])
        return jnp.concatenate(parts, axis=0)

    def halo_tiles(ps, hs):
        for p, h in zip(ps, hs):
            w = slot(p)
            near = win[pl.ds(w - REACH, 2 * REACH + 1)].reshape((2 * REACH + 1) * TILE, TILE)
            acc = jnp.dot(halo_a[h], near, preferred_element_type=jnp.float32)
            fresh[local(p) + REACH] = acc.astype(jnp.bfloat16)

    def gradient(t, u):
        g = lax.dot_general(
            left_v[rows(t), :], picked(t), (((1,), (1,)), ((), ())), preferred_element_type=jnp.float32
        )
        for j in range(pairs):
            wide[u, pl.ds(j, TILE, stride=pairs), :] = g[:, j * TILE:(j + 1) * TILE]
        grad_v[mixed(t), :] = wide[u].astype(jnp.bfloat16)

    @pl.when(has_pre)
    def _():
        for u in range(REACH):
            arrive(-1 - u)

        @pl.when(wider)
        def _():
            for u in range(REACH, EDGE):
                arrive(-1 - u)

    for u in range(REACH):
        take(u)

    def halo_ready(hs):
        for h in hs:
            pltpu.make_async_copy(halo_a.at[h], halo_a.at[h], halo_sem.at[h]).wait()

    sends_edges = jnp.logical_and(col > 0, jnp.logical_not(wider))
    out_reach = jnp.where(first, REACH, EDGE)

    def own_tile(t):
        acc = jnp.dot(a_v[rows(t), :], picked(t), preferred_element_type=jnp.float32)
        fresh[t + REACH] = acc.astype(jnp.bfloat16)

    def pass_on(p):
        @pl.when(jnp.logical_and(jnp.logical_and(p < out_reach, has_pre), sends_edges))
        def _():
            send_pre(held(p), p, col - 1, 0).start()

        @pl.when(jnp.logical_and(jnp.logical_and(p >= tiles - out_reach, has_post), sends_edges))
        def _():
            send_post(held(p), p, col - 1, 0).start()

        @pl.when(col > 0)
        def _():
            send_on(p).start()

    early = jnp.logical_and(wider, has_pre)
    last = tiles - REACH

    @pl.when(early)
    def _():
        take(REACH)
        halo_ready((0, 1))
        halo_tiles((-2, -1), (1, 0))
        own_tile(local(0))
        send_on(-2, 0).start()
        send_on(-1, 1).start()
        send_on(0).start()

    def step(p, carry):
        t = local(p)

        @pl.when(jnp.logical_and(first, p % GROUP == 0))
        def _():
            sort_group(p // GROUP)

        take(p + REACH)
        own_tile(t)
        pass_on(p)

        @pl.when(jnp.logical_and(col == 0, t % 2 == 1))
        def _():
            gradient(t, 0)

        return carry

    lax.fori_loop(count(early), last, step, 0)

    @pl.when(has_post)
    def _():
        arrive(tiles)
        arrive(tiles + 1)

    late = jnp.logical_and(wider, has_post)

    @pl.when(late)
    def _():
        arrive(tiles + 2)
        arrive(tiles + 3)
        halo_ready((2, 3))
        own_tile(local(last))
        own_tile(local(last + 1))
        halo_tiles((tiles, tiles + 1), (2, 3))
        send_on(last).start()
        send_on(last + 1).start()
        send_on(tiles, 3).start()
        send_on(tiles + 1, 4).start()

    @pl.when(jnp.logical_not(late))
    def _():
        own_tile(local(last))
        own_tile(local(last + 1))
        pass_on(last)
        pass_on(last + 1)

    store_env.start()

    @pl.when(col > 0)
    def _():
        def four(i, carry):
            for u in range(4):
                gradient(4 * i + u, u)
            store_grad(i).start()
            return carry

        lax.fori_loop(0, tiles // 4, four, 0)

    @pl.when(col == 0)
    def _():
        gradient(local(last + 1 - odd), 0)

        def four(i, carry):
            for u in range(4):
                gradient(8 * i + 2 * u, u)
            store_grad(2 * i).start()
            store_grad(2 * i + 1).start()
            return carry

        lax.fori_loop(0, tiles // 8, four, 0)

    @pl.when(col > 0)
    def _():
        main = fresh.at[pl.ds(REACH, tiles)]
        pltpu.make_async_copy(main, main, send_sem.at[REACH]).wait()

    for there, at, own in ((has_pre, -REACH, 0), (has_post, tiles, 3)):
        @pl.when(jnp.logical_and(wider, there))
        def _():
            for u in range(REACH):
                send_on(at + u, own + u).wait_send()

    edge_spreads(lambda p, copy: copy.wait_send())

    for u in range(EDGE):
        sent_edge = jnp.logical_and(sends_edges, u < out_reach)

        @pl.when(jnp.logical_and(sent_edge, has_pre))
        def _():
            send_pre(held(u), u, col - 1, 0).wait_send()

        @pl.when(jnp.logical_and(sent_edge, has_post))
        def _():
            send_post(held(tiles - 1 - u), tiles - 1 - u, col - 1, 0).wait_send()

    first_edges(lambda copy: copy.wait_send())
    store_env.wait()

    def stored(i, carry):
        store_grad(i).wait()
        return carry

    lax.fori_loop(0, tiles // 4, stored, 0)


def per_device(env_right, transfer, sources, env_left):
    ncol = lax.axis_size("col")
    nsec = lax.axis_size("sec")
    length = transfer.shape[2]
    pairs = transfer.shape[3]
    width = env_right.shape[2]
    tiles = length // TILE
    b = transfer.reshape(length * pairs, TILE)
    left = env_left.reshape(length, width)
    src = jnp.transpose(sources.reshape(tiles, pairs))
    bf16 = jnp.bfloat16
    in_hbm = pl.BlockSpec(memory_space=pltpu.HBM)
    anywhere = pl.BlockSpec(memory_space=pl.ANY)
    dma = pltpu.SemaphoreType.DMA
    env, grad = pl.pallas_call(
        functools.partial(sweep_kernel, ncol, nsec, pairs),
        out_shape=(
            jax.ShapeDtypeStruct((tiles, TILE, width), bf16),
            jax.ShapeDtypeStruct((length * pairs, TILE), bf16),
        ),
        in_specs=[pl.BlockSpec(memory_space=pltpu.SMEM), in_hbm, in_hbm, in_hbm],
        out_specs=(anywhere, anywhere),
        scratch_shapes=[
            pltpu.VMEM((length * pairs, TILE), bf16),
            pltpu.VMEM((length, pairs * TILE), bf16),
            pltpu.VMEM((length, width), bf16),
            pltpu.VMEM((length, width), bf16),
            pltpu.VMEM((tiles + 2 * EDGE, TILE, width), bf16),
            pltpu.VMEM((tiles + 2 * EDGE, TILE, width), bf16),
            pltpu.VMEM((tiles + 2 * REACH, TILE, width), bf16),
            pltpu.VMEM((length * pairs, TILE), bf16),
            pltpu.VMEM((4, pairs * TILE, TILE), jnp.float32),
            pltpu.VMEM((2 * REACH, TILE, (2 * REACH + 1) * TILE), bf16),
            pltpu.VMEM((2 * REACH, TILE, (2 * REACH + 1) * TILE), bf16),
            dma((tiles + 2 * EDGE,)),
            dma((2 * REACH + 1 + 4 * EDGE,)),
            dma((tiles // GROUP,)),
            dma,
            dma,
            dma,
            dma((tiles // 4,)),
            dma((2 * REACH,)),
            dma((2 * REACH,)),
        ],
        compiler_params=pltpu.CompilerParams(
            collective_id=0, has_side_effects=True, vmem_limit_bytes=24 * 1024 * 1024
        ),
        name="sweep",
    )(src, *(pltpu.with_memory_space_constraint(x, pltpu.HBM) for x in (env_right.reshape(length, width), b, left)))
    return env.reshape(1, 1, length, width), grad.reshape(1, 1, length, pairs, TILE)


def solution(mesh):
    placed = (
        P(None, "sec", None),
        P("col", None, "sec", None, None),
        P("col", None, "sec", None),
        P("col", None, "sec", None),
    )
    return jax.shard_map(
        per_device,
        mesh=mesh,
        in_specs=placed,
        out_specs=(P("col", None, "sec", None), P("col", None, "sec", None, None)),
        check_vma=False,
    )
```

```python
import functools

import jax
import jax.numpy as jnp
from jax import lax
from jax.experimental import pallas as pl
from jax.experimental.pallas import tpu as pltpu
from jax.sharding import PartitionSpec as P

TILE = 128
REACH = 2
EDGE = 2 * REACH
GROUP = 4
MESH = pl.DeviceIdType.MESH


def sweep_kernel(
    ncol, nsec, pairs, src_hbm, env_hbm, b_hbm, left_hbm, env_out, grad_out,
    src_ref, b_v, a_v, left_v, env_v, land, win, fresh, grad_v, wide, spread, halo_a,
    src_sem, recv_sem, send_sem, b_sem, left_sem, env_sem, out_sem, gout_sem, spread_sem, halo_sem,
):
    col = lax.axis_index("col")
    sec = lax.axis_index("sec")
    tiles = left_v.shape[0] // TILE
    groups = tiles // GROUP
    odd = 1 - sec % 2
    first = col == ncol - 1
    wider = jnp.logical_and(col % 2 == 1, jnp.logical_not(first))
    has_below = sec > 0
    has_above = sec < nsec - 1
    side = 2 * odd - 1
    has_pre = jnp.logical_and(sec + side >= 0, sec + side < nsec)
    has_post = jnp.logical_and(sec - side >= 0, sec - side < nsec)

    def local(p):
        return p + odd * (tiles - 1 - 2 * p)

    def slot(p):
        return local(p) + EDGE

    def slot_beside(p):
        return tiles - 1 - p + odd * (2 * p + 1 - tiles) + EDGE

    def rows(t):
        return pl.ds(pl.multiple_of(t * TILE, TILE), TILE)

    def mixed(t, n=1):
        return pl.ds(pl.multiple_of(t * pairs * TILE, pairs * TILE), n * pairs * TILE)

    def load_b(g):
        span = mixed(g * GROUP, GROUP)
        return pltpu.make_async_copy(b_hbm.at[span], b_v.at[span], b_sem.at[g])

    load_src = pltpu.make_async_copy(src_hbm, src_ref, src_sem)
    load_left = pltpu.make_async_copy(left_hbm, left_v, left_sem)
    load_env = pltpu.make_async_copy(env_hbm, env_v, env_sem)
    store_env = pltpu.make_async_copy(fresh.at[pl.ds(REACH, tiles)], env_out, out_sem)

    def store_grad(i):
        span = mixed(4 * i, 4)
        return pltpu.make_async_copy(grad_v.at[span], grad_out.at[span], gout_sem.at[i])

    def send(src, w, sem, to_col, to_sec):
        return pltpu.make_async_remote_copy(
            src_ref=src,
            dst_ref=land.at[w],
            send_sem=send_sem.at[sem],
            recv_sem=recv_sem.at[w],
            device_id=(to_col, to_sec),
            device_id_type=MESH,
        )

    def held(p):
        return fresh.at[local(p) + REACH]

    def send_on(p, own=None):
        return send(held(p), slot(p), REACH if own is None else own, col - 1, sec)

    after = 2 * REACH + 1

    def send_pre(src, p, to_col, at):
        return send(src, slot_beside(-1 - p), after + at + p, to_col, sec + side)

    def send_post(src, p, to_col, at):
        return send(src, slot_beside(2 * tiles - 1 - p), after + at + EDGE + tiles - 1 - p, to_col, sec - side)

    def send_spread(h, to_sec):
        return pltpu.make_async_remote_copy(
            src_ref=spread.at[h],
            dst_ref=halo_a.at[h],
            send_sem=spread_sem.at[h],
            recv_sem=halo_sem.at[h],
            device_id=(col, to_sec),
            device_id_type=MESH,
        )

    barrier = pltpu.get_barrier_semaphore()

    def greet(to_col, to_sec):
        pl.semaphore_signal(barrier, inc=1, device_id=(to_col, to_sec), device_id_type=MESH)

    @pl.when(jnp.logical_not(first))
    def _():
        greet(col + 1, sec)

    behind = jnp.minimum(col + 1, ncol - 1)
    meets = jnp.logical_or(col % 2 == 1, col == ncol - 2)
    for there, by in ((has_below, -1), (has_above, 1)):
        @pl.when(jnp.logical_and(there, meets))
        def _():
            greet(behind, sec + by)

        @pl.when(jnp.logical_and(there, wider))
        def _():
            greet(col, sec + by)

    load_src.start()

    @pl.when(first)
    def _():
        load_env.start()

    def start_loads(i, carry):
        load_b(i + odd * (groups - 1 - 2 * i)).start()
        return carry

    lax.fori_loop(0, groups, start_loads, 0)
    load_left.start()

    def count(flag):
        return flag.astype(jnp.int32)

    beside = count(has_below) + count(has_above)

    @pl.when(col > 0)
    def _():
        pl.semaphore_wait(barrier, 1 + beside + count(first) * beside)

    def first_edges(do):
        @pl.when(jnp.logical_and(first, has_pre))
        def _():
            for u in range(REACH):
                do(send_pre(env_hbm.at[rows(local(u))], u, col, 2 * EDGE))

        @pl.when(jnp.logical_and(first, has_post))
        def _():
            for u in range(REACH):
                p = tiles - 1 - u
                do(send_post(env_hbm.at[rows(local(p))], p, col, 2 * EDGE))

    first_edges(lambda copy: copy.start())
    win[...] = jnp.zeros_like(win)
    load_src.wait()

    def sort_rows(t):
        wide[0] = b_v[mixed(t), :].astype(jnp.float32)
        for j in range(pairs):
            part = wide[0, pl.ds(j, TILE, stride=pairs), :]
            a_v[rows(t), j * TILE:(j + 1) * TILE] = part.astype(jnp.bfloat16)

    def sort_group(i):
        g = i + odd * (groups - 1 - 2 * i)
        load_b(g).wait()
        for u in range(GROUP):
            sort_rows(g * GROUP + u)

    def by_offset(t, h):
        blocks = [a_v[rows(t), j * TILE:(j + 1) * TILE].astype(jnp.float32) for j in range(pairs)]
        for k in range(2 * REACH + 1):
            total = jnp.zeros((TILE, TILE), jnp.float32)
            for j in range(pairs):
                here = src_ref[j, t] - sec * tiles - t == k - REACH
                total = total + jnp.where(here, blocks[j], 0.0)
            spread[h, :, k * TILE:(k + 1) * TILE] = total.astype(jnp.bfloat16)

    def edge_spreads(do):
        @pl.when(jnp.logical_and(wider, has_pre))
        def _():
            for u in range(REACH):
                do(u, send_spread(u, sec + side))

        @pl.when(jnp.logical_and(wider, has_post))
        def _():
            for u in range(REACH):
                do(tiles - 1 - u, send_spread(REACH + u, sec - side))

    @pl.when(jnp.logical_not(first))
    def _():
        sort_group(0)
        sort_group(groups - 1)

        @pl.when(wider)
        def _():
            for u in range(REACH):
                by_offset(local(u), u)
                by_offset(local(tiles - 1 - u), REACH + u)

        edge_spreads(lambda p, copy: copy.start())

        def one(i, carry):
            sort_group(i)
            return carry

        lax.fori_loop(1, groups - 1, one, 0)

    load_left.wait()

    def arrive(p):
        w = slot(p)
        pltpu.make_async_copy(land.at[w], land.at[w], recv_sem.at[w]).wait()
        win[w] = land[w]

    def take(p):
        @pl.when(first)
        def _():
            from_start(p)

        @pl.when(jnp.logical_not(first))
        def _():
            arrive(p)

    def picked(t):
        parts = []
        for j in range(pairs):
            i = src_ref[j, t] - sec * tiles + EDGE
            parts.append(win[jnp.clip(i, 0, win.shape[0] - 1)])
        return jnp.concatenate(parts, axis=0)

    def halo_tiles(ps, hs):
        for p, h in zip(ps, hs):
            w = slot(p)
            near = win[pl.ds(w - REACH, 2 * REACH + 1)].reshape((2 * REACH + 1) * TILE, TILE)
            acc = jnp.dot(halo_a[h], near, preferred_element_type=jnp.float32)
            fresh[local(p) + REACH] = acc.astype(jnp.bfloat16)

    def gradient(t, u):
        g = lax.dot_general(
            left_v[rows(t), :], picked(t), (((1,), (1,)), ((), ())), preferred_element_type=jnp.float32
        )
        for j in range(pairs):
            wide[u, pl.ds(j, TILE, stride=pairs), :] = g[:, j * TILE:(j + 1) * TILE]
        grad_v[mixed(t), :] = wide[u].astype(jnp.bfloat16)

    def own_tile(t):
        acc = jnp.dot(a_v[rows(t), :], picked(t), preferred_element_type=jnp.float32)
        fresh[t + REACH] = acc.astype(jnp.bfloat16)

    def from_start(p):
        win[slot(p)] = env_v[rows(local(p)), :]

    @pl.when(first)
    def _():
        load_env.wait()
        sort_group(0)
        for p in range(GROUP + REACH):
            from_start(p)
        for p in range(REACH, GROUP):
            own_tile(local(p))

    @pl.when(has_pre)
    def _():
        for u in range(REACH):
            arrive(-1 - u)

        @pl.when(wider)
        def _():
            for u in range(REACH, EDGE):
                arrive(-1 - u)

    @pl.when(jnp.logical_not(first))
    def _():
        for u in range(REACH):
            arrive(u)

    def halo_ready(hs):
        for h in hs:
            pltpu.make_async_copy(halo_a.at[h], halo_a.at[h], halo_sem.at[h]).wait()

    sends_edges = jnp.logical_and(col > 0, jnp.logical_not(wider))
    out_reach = jnp.where(first, REACH, EDGE)

    ahead_pre = jnp.logical_and(jnp.logical_and(sends_edges, has_pre), jnp.logical_not(first))
    ahead_post = jnp.logical_and(jnp.logical_and(sends_edges, has_post), jnp.logical_not(first))

    def pass_on(p):
        @pl.when(jnp.logical_and(jnp.logical_and(p < out_reach, has_pre), sends_edges))
        def _():
            send_pre(held(p), p, col - 1, 0).start()

        @pl.when(jnp.logical_and(jnp.logical_and(p >= tiles - out_reach, has_post), sends_edges))
        def _():
            send_post(held(p), p, col - 1, 0).start()

        behind_pre = jnp.logical_and(ahead_pre, p < EDGE)
        behind_post = jnp.logical_and(ahead_post, p >= tiles - EDGE)

        @pl.when(jnp.logical_or(jnp.logical_and(behind_pre, p > 0), jnp.logical_and(behind_post, p > tiles - EDGE)))
        def _():
            send_on(p - 1).start()

        held_back = jnp.logical_or(jnp.logical_and(behind_pre, p < EDGE - 1), jnp.logical_and(behind_post, p < tiles - 1))

        @pl.when(jnp.logical_and(col > 0, jnp.logical_not(held_back)))
        def _():
            send_on(p).start()

    early = jnp.logical_and(wider, has_pre)
    last = tiles - REACH

    @pl.when(first)
    def _():
        for p in range(REACH):
            own_tile(local(p))
        for p in range(GROUP):
            pass_on(p)

    @pl.when(early)
    def _():
        arrive(REACH)
        halo_ready((0, 1))
        halo_tiles((-2, -1), (1, 0))
        own_tile(local(0))
        send_on(-2, 0).start()
        send_on(-1, 1).start()
        send_on(0).start()

    def step(p, carry):
        t = local(p)

        @pl.when(jnp.logical_and(first, p % GROUP == 0))
        def _():
            sort_group(p // GROUP)

        take(p + REACH)
        own_tile(t)
        pass_on(p)

        @pl.when(jnp.logical_and(col == 0, t % 2 == 1))
        def _():
            gradient(t, 0)

        return carry

    lax.fori_loop(count(early) + GROUP * count(first), last, step, 0)

    @pl.when(has_post)
    def _():
        arrive(tiles)
        arrive(tiles + 1)

    late = jnp.logical_and(wider, has_post)

    @pl.when(late)
    def _():
        arrive(tiles + 2)
        arrive(tiles + 3)
        halo_ready((2, 3))
        own_tile(local(last))
        own_tile(local(last + 1))
        halo_tiles((tiles, tiles + 1), (2, 3))
        send_on(last).start()
        send_on(last + 1).start()
        send_on(tiles, 3).start()
        send_on(tiles + 1, 4).start()

    @pl.when(jnp.logical_not(late))
    def _():
        own_tile(local(last))
        own_tile(local(last + 1))

        @pl.when(ahead_post)
        def _():
            send_post(held(last), last, col - 1, 0).start()
            send_post(held(last + 1), last + 1, col - 1, 0).start()
            for p in range(last - 1, tiles):
                send_on(p).start()

        @pl.when(jnp.logical_not(ahead_post))
        def _():
            pass_on(last)
            pass_on(last + 1)

    store_env.start()

    @pl.when(col > 0)
    def _():
        def four(i, carry):
            for u in range(4):
                gradient(4 * i + u, u)
            store_grad(i).start()
            return carry

        lax.fori_loop(0, tiles // 4, four, 0)

    @pl.when(col == 0)
    def _():
        gradient(local(last + 1 - odd), 0)

        def four(i, carry):
            for u in range(4):
                gradient(8 * i + 2 * u, u)
            store_grad(2 * i).start()
            store_grad(2 * i + 1).start()
            return carry

        lax.fori_loop(0, tiles // 8, four, 0)

    @pl.when(col > 0)
    def _():
        main = fresh.at[pl.ds(REACH, tiles)]
        pltpu.make_async_copy(main, main, send_sem.at[REACH]).wait()

    for there, at, own in ((has_pre, -REACH, 0), (has_post, tiles, 3)):
        @pl.when(jnp.logical_and(wider, there))
        def _():
            for u in range(REACH):
                send_on(at + u, own + u).wait_send()

    edge_spreads(lambda p, copy: copy.wait_send())

    for u in range(EDGE):
        sent_edge = jnp.logical_and(sends_edges, u < out_reach)

        @pl.when(jnp.logical_and(sent_edge, has_pre))
        def _():
            send_pre(held(u), u, col - 1, 0).wait_send()

        @pl.when(jnp.logical_and(sent_edge, has_post))
        def _():
            send_post(held(tiles - 1 - u), tiles - 1 - u, col - 1, 0).wait_send()

    first_edges(lambda copy: copy.wait_send())
    store_env.wait()

    def stored(i, carry):
        store_grad(i).wait()
        return carry

    lax.fori_loop(0, tiles // 4, stored, 0)


def per_device(env_right, transfer, sources, env_left):
    ncol = lax.axis_size("col")
    nsec = lax.axis_size("sec")
    length = transfer.shape[2]
    pairs = transfer.shape[3]
    width = env_right.shape[2]
    tiles = length // TILE
    b = transfer.reshape(length * pairs, TILE)
    left = env_left.reshape(length, width)
    src = jnp.transpose(sources.reshape(tiles, pairs))
    bf16 = jnp.bfloat16
    in_hbm = pl.BlockSpec(memory_space=pltpu.HBM)
    anywhere = pl.BlockSpec(memory_space=pl.ANY)
    dma = pltpu.SemaphoreType.DMA
    env, grad = pl.pallas_call(
        functools.partial(sweep_kernel, ncol, nsec, pairs),
        out_shape=(
            jax.ShapeDtypeStruct((tiles, TILE, width), bf16),
            jax.ShapeDtypeStruct((length * pairs, TILE), bf16),
        ),
        in_specs=[in_hbm, in_hbm, in_hbm, in_hbm],
        out_specs=(anywhere, anywhere),
        scratch_shapes=[
            pltpu.SMEM((pairs, tiles), jnp.int32),
            pltpu.VMEM((length * pairs, TILE), bf16),
            pltpu.VMEM((length, pairs * TILE), bf16),
            pltpu.VMEM((length, width), bf16),
            pltpu.VMEM((length, width), bf16),
            pltpu.VMEM((tiles + 2 * EDGE, TILE, width), bf16),
            pltpu.VMEM((tiles + 2 * EDGE, TILE, width), bf16),
            pltpu.VMEM((tiles + 2 * REACH, TILE, width), bf16),
            pltpu.VMEM((length * pairs, TILE), bf16),
            pltpu.VMEM((4, pairs * TILE, TILE), jnp.float32),
            pltpu.VMEM((2 * REACH, TILE, (2 * REACH + 1) * TILE), bf16),
            pltpu.VMEM((2 * REACH, TILE, (2 * REACH + 1) * TILE), bf16),
            dma,
            dma((tiles + 2 * EDGE,)),
            dma((2 * REACH + 1 + 4 * EDGE,)),
            dma((tiles // GROUP,)),
            dma,
            dma,
            dma,
            dma((tiles // 4,)),
            dma((2 * REACH,)),
            dma((2 * REACH,)),
        ],
        compiler_params=pltpu.CompilerParams(
            collective_id=0, has_side_effects=True, vmem_limit_bytes=24 * 1024 * 1024
        ),
        name="sweep",
    )(*(pltpu.with_memory_space_constraint(x, pltpu.HBM) for x in (src, env_right.reshape(length, width), b, left)))
    return env.reshape(1, 1, length, width), grad.reshape(1, 1, length, pairs, TILE)


def solution(mesh):
    placed = (
        P(None, "sec", None),
        P("col", None, "sec", None, None),
        P("col", None, "sec", None),
        P("col", None, "sec", None),
    )
    return jax.shard_map(
        per_device,
        mesh=mesh,
        in_specs=placed,
        out_specs=(P("col", None, "sec", None), P("col", None, "sec", None, None)),
        check_vma=False,
    )
```

```python
import functools

import jax
import jax.numpy as jnp
from jax import lax
from jax.experimental import pallas as pl
from jax.experimental.pallas import tpu as pltpu
from jax.sharding import PartitionSpec as P

TILE = 128
REACH = 2
EDGE = 2 * REACH
GROUP = 4
EARLY = 3
MESH = pl.DeviceIdType.MESH


def sweep_kernel(
    ncol, nsec, pairs, src_hbm, env_hbm, b_hbm, left_hbm, env_out, grad_out,
    src_ref, b_v, a_v, left_v, env_v, land, win, fresh, grad_v, wide, spread, halo_a,
    src_sem, recv_sem, send_sem, b_sem, left_sem, env_sem, out_sem, gout_sem, spread_sem, halo_sem,
):
    col = lax.axis_index("col")
    sec = lax.axis_index("sec")
    tiles = left_v.shape[0] // TILE
    groups = tiles // GROUP
    odd = 1 - sec % 2
    first = col == ncol - 1
    wider = jnp.logical_and(col % 2 == 1, jnp.logical_not(first))
    has_below = sec > 0
    has_above = sec < nsec - 1
    side = 2 * odd - 1
    has_pre = jnp.logical_and(sec + side >= 0, sec + side < nsec)
    has_post = jnp.logical_and(sec - side >= 0, sec - side < nsec)

    def local(p):
        return p + odd * (tiles - 1 - 2 * p)

    def slot(p):
        return local(p) + EDGE

    def slot_beside(p):
        return tiles - 1 - p + odd * (2 * p + 1 - tiles) + EDGE

    def rows(t):
        return pl.ds(pl.multiple_of(t * TILE, TILE), TILE)

    def mixed(t, n=1):
        return pl.ds(pl.multiple_of(t * pairs * TILE, pairs * TILE), n * pairs * TILE)

    def load_b(g):
        span = mixed(g * GROUP, GROUP)
        return pltpu.make_async_copy(b_hbm.at[span], b_v.at[span], b_sem.at[g])

    load_src = pltpu.make_async_copy(src_hbm, src_ref, src_sem)
    load_left = pltpu.make_async_copy(left_hbm, left_v, left_sem)
    load_env = pltpu.make_async_copy(env_hbm, env_v, env_sem)
    store_env = pltpu.make_async_copy(fresh.at[pl.ds(REACH, tiles)], env_out, out_sem)

    def store_grad(i):
        span = mixed(4 * i, 4)
        return pltpu.make_async_copy(grad_v.at[span], grad_out.at[span], gout_sem.at[i])

    def send(src, w, sem, to_col, to_sec):
        return pltpu.make_async_remote_copy(
            src_ref=src,
            dst_ref=land.at[w],
            send_sem=send_sem.at[sem],
            recv_sem=recv_sem.at[w],
            device_id=(to_col, to_sec),
            device_id_type=MESH,
        )

    def held(p):
        return fresh.at[local(p) + REACH]

    def send_on(p, own=None):
        return send(held(p), slot(p), REACH if own is None else own, col - 1, sec)

    after = 2 * REACH + 1

    def send_pre(src, p, to_col, at):
        return send(src, slot_beside(-1 - p), after + at + p, to_col, sec + side)

    def send_post(src, p, to_col, at):
        return send(src, slot_beside(2 * tiles - 1 - p), after + at + EDGE + tiles - 1 - p, to_col, sec - side)

    def send_spread(h, to_sec):
        return pltpu.make_async_remote_copy(
            src_ref=spread.at[h],
            dst_ref=halo_a.at[h],
            send_sem=spread_sem.at[h],
            recv_sem=halo_sem.at[h],
            device_id=(col, to_sec),
            device_id_type=MESH,
        )

    barrier = pltpu.get_barrier_semaphore()

    def greet(to_col, to_sec):
        pl.semaphore_signal(barrier, inc=1, device_id=(to_col, to_sec), device_id_type=MESH)

    @pl.when(jnp.logical_not(first))
    def _():
        greet(col + 1, sec)

    behind = jnp.minimum(col + 1, ncol - 1)
    meets = jnp.logical_or(col % 2 == 1, col == ncol - 2)
    for there, by in ((has_below, -1), (has_above, 1)):
        @pl.when(jnp.logical_and(there, meets))
        def _():
            greet(behind, sec + by)

        @pl.when(jnp.logical_and(there, wider))
        def _():
            greet(col, sec + by)

    load_src.start()

    @pl.when(first)
    def _():
        load_env.start()

    def start_loads(i, carry):
        load_b(i + odd * (groups - 1 - 2 * i)).start()
        return carry

    lax.fori_loop(0, groups, start_loads, 0)
    load_left.start()

    def count(flag):
        return flag.astype(jnp.int32)

    beside = count(has_below) + count(has_above)

    @pl.when(col > 0)
    def _():
        pl.semaphore_wait(barrier, 1 + beside + count(first) * beside)

    def first_edges(do):
        @pl.when(jnp.logical_and(first, has_pre))
        def _():
            for u in range(REACH):
                do(send_pre(env_hbm.at[rows(local(u))], u, col, 2 * EDGE))

        @pl.when(jnp.logical_and(first, has_post))
        def _():
            for u in range(REACH):
                p = tiles - 1 - u
                do(send_post(env_hbm.at[rows(local(p))], p, col, 2 * EDGE))

    first_edges(lambda copy: copy.start())
    win[...] = jnp.zeros_like(win)
    load_src.wait()

    def sort_rows(t):
        wide[0] = b_v[mixed(t), :].astype(jnp.float32)
        for j in range(pairs):
            part = wide[0, pl.ds(j, TILE, stride=pairs), :]
            a_v[rows(t), j * TILE:(j + 1) * TILE] = part.astype(jnp.bfloat16)

    def sort_group(i):
        g = i + odd * (groups - 1 - 2 * i)
        load_b(g).wait()
        for u in range(GROUP):
            sort_rows(g * GROUP + u)

    def by_offset(t, h):
        blocks = [a_v[rows(t), j * TILE:(j + 1) * TILE].astype(jnp.float32) for j in range(pairs)]
        for k in range(2 * REACH + 1):
            total = jnp.zeros((TILE, TILE), jnp.float32)
            for j in range(pairs):
                here = src_ref[j, t] - sec * tiles - t == k - REACH
                total = total + jnp.where(here, blocks[j], 0.0)
            spread[h, :, k * TILE:(k + 1) * TILE] = total.astype(jnp.bfloat16)

    def edge_spreads(do):
        @pl.when(jnp.logical_and(wider, has_pre))
        def _():
            for u in range(REACH):
                do(u, send_spread(u, sec + side))

        @pl.when(jnp.logical_and(wider, has_post))
        def _():
            for u in range(REACH):
                do(tiles - 1 - u, send_spread(REACH + u, sec - side))

    @pl.when(jnp.logical_not(first))
    def _():
        sort_group(0)
        sort_group(groups - 1)

        @pl.when(wider)
        def _():
            for u in range(REACH):
                by_offset(local(u), u)
                by_offset(local(tiles - 1 - u), REACH + u)

        edge_spreads(lambda p, copy: copy.start())

        def one(i, carry):
            sort_group(i)
            return carry

        lax.fori_loop(1, groups - 1, one, 0)

    load_left.wait()

    def arrive(p):
        w = slot(p)
        pltpu.make_async_copy(land.at[w], land.at[w], recv_sem.at[w]).wait()
        win[w] = land[w]

    def take(p):
        @pl.when(first)
        def _():
            from_start(p)

        @pl.when(jnp.logical_not(first))
        def _():
            arrive(p)

    def picked(t):
        parts = []
        for j in range(pairs):
            i = src_ref[j, t] - sec * tiles + EDGE
            parts.append(win[jnp.clip(i, 0, win.shape[0] - 1)])
        return jnp.concatenate(parts, axis=0)

    def halo_tiles(ps, hs):
        for p, h in zip(ps, hs):
            w = slot(p)
            near = win[pl.ds(w - REACH, 2 * REACH + 1)].reshape((2 * REACH + 1) * TILE, TILE)
            acc = jnp.dot(halo_a[h], near, preferred_element_type=jnp.float32)
            fresh[local(p) + REACH] = acc.astype(jnp.bfloat16)

    def gradient(t, u):
        g = lax.dot_general(
            left_v[rows(t), :], picked(t), (((1,), (1,)), ((), ())), preferred_element_type=jnp.float32
        )
        for j in range(pairs):
            wide[u, pl.ds(j, TILE, stride=pairs), :] = g[:, j * TILE:(j + 1) * TILE]
        grad_v[mixed(t), :] = wide[u].astype(jnp.bfloat16)

    def own_tile(t):
        acc = jnp.dot(a_v[rows(t), :], picked(t), preferred_element_type=jnp.float32)
        fresh[t + REACH] = acc.astype(jnp.bfloat16)

    def from_start(p):
        win[slot(p)] = env_v[rows(local(p)), :]

    @pl.when(first)
    def _():
        load_env.wait()
        sort_group(0)
        for p in range(GROUP + REACH):
            from_start(p)
        for p in range(REACH, GROUP):
            own_tile(local(p))

    @pl.when(has_pre)
    def _():
        for u in range(REACH):
            arrive(-1 - u)

        @pl.when(wider)
        def _():
            for u in range(REACH, EDGE):
                arrive(-1 - u)

    @pl.when(jnp.logical_not(first))
    def _():
        for u in range(REACH):
            arrive(u)

    def halo_ready(hs):
        for h in hs:
            pltpu.make_async_copy(halo_a.at[h], halo_a.at[h], halo_sem.at[h]).wait()

    sends_edges = jnp.logical_and(col > 0, jnp.logical_not(wider))
    out_reach = jnp.where(first, REACH, EDGE)

    ahead_pre = jnp.logical_and(jnp.logical_and(sends_edges, has_pre), jnp.logical_not(first))
    ahead_post = jnp.logical_and(jnp.logical_and(sends_edges, has_post), jnp.logical_not(first))

    def pass_on(p):
        @pl.when(jnp.logical_and(jnp.logical_and(p < out_reach, has_pre), sends_edges))
        def _():
            send_pre(held(p), p, col - 1, 0).start()

        @pl.when(jnp.logical_and(jnp.logical_and(p >= tiles - out_reach, has_post), sends_edges))
        def _():
            send_post(held(p), p, col - 1, 0).start()

        behind_pre = jnp.logical_and(ahead_pre, p < EDGE)
        behind_post = jnp.logical_and(ahead_post, p >= tiles - EDGE)

        @pl.when(jnp.logical_or(jnp.logical_and(behind_pre, p > 0), jnp.logical_and(behind_post, p > tiles - EDGE)))
        def _():
            send_on(p - 1).start()

        held_back = jnp.logical_or(jnp.logical_and(behind_pre, p < EDGE - 1), jnp.logical_and(behind_post, p < tiles - 1))

        @pl.when(jnp.logical_and(col > 0, jnp.logical_not(held_back)))
        def _():
            send_on(p).start()

    early = jnp.logical_and(wider, has_pre)
    last = tiles - REACH

    @pl.when(first)
    def _():
        for p in range(REACH):
            own_tile(local(p))
        for p in range(GROUP):
            pass_on(p)

    @pl.when(early)
    def _():
        arrive(REACH)
        halo_ready((0, 1))
        halo_tiles((-2, -1), (1, 0))
        own_tile(local(0))
        send_on(-2, 0).start()
        send_on(-1, 1).start()
        send_on(0).start()
        arrive(REACH + 1)
        arrive(REACH + 2)
        own_tile(local(1))
        own_tile(local(2))
        send_on(1).start()
        send_on(2).start()

    nearby = col < 2

    def step(p, carry):
        t = local(p)

        @pl.when(jnp.logical_and(first, p % GROUP == 0))
        def _():
            sort_group(p // GROUP)

        take(p + REACH)
        @pl.when(nearby)
        def _():
            own_tile(t)
            gradient(t, 0)

        @pl.when(jnp.logical_not(nearby))
        def _():
            own_tile(t)

        pass_on(p)

        @pl.when(jnp.logical_and(jnp.logical_and(nearby, p % GROUP == GROUP - 1), p >= GROUP))
        def _():
            store_grad(t // GROUP).start()

        return carry

    lax.fori_loop(EARLY * count(early) + GROUP * count(first), last, step, 0)

    @pl.when(has_post)
    def _():
        arrive(tiles)
        arrive(tiles + 1)

    late = jnp.logical_and(wider, has_post)

    @pl.when(late)
    def _():
        arrive(tiles + 2)
        arrive(tiles + 3)
        halo_ready((2, 3))
        own_tile(local(last))
        own_tile(local(last + 1))
        halo_tiles((tiles, tiles + 1), (2, 3))
        send_on(last).start()
        send_on(last + 1).start()
        send_on(tiles, 3).start()
        send_on(tiles + 1, 4).start()

    @pl.when(jnp.logical_not(late))
    def _():
        own_tile(local(last))
        own_tile(local(last + 1))

        @pl.when(ahead_post)
        def _():
            send_post(held(last), last, col - 1, 0).start()
            send_post(held(last + 1), last + 1, col - 1, 0).start()
            for p in range(last - 1, tiles):
                send_on(p).start()

        @pl.when(jnp.logical_not(ahead_post))
        def _():
            pass_on(last)
            pass_on(last + 1)

    store_env.start()

    @pl.when(jnp.logical_not(nearby))
    def _():
        def four(i, carry):
            for u in range(GROUP):
                gradient(GROUP * i + u, u)
            store_grad(i).start()
            return carry

        lax.fori_loop(0, groups, four, 0)

    @pl.when(nearby)
    def _():
        for u in range(EARLY):
            gradient(local(u), u)
        store_grad(local(0) // GROUP).start()
        for u in range(REACH):
            gradient(local(last + u), u)
        store_grad(local(last) // GROUP).start()

    @pl.when(col > 0)
    def _():
        main = fresh.at[pl.ds(REACH, tiles)]
        pltpu.make_async_copy(main, main, send_sem.at[REACH]).wait()

    for there, at, own in ((has_pre, -REACH, 0), (has_post, tiles, 3)):
        @pl.when(jnp.logical_and(wider, there))
        def _():
            for u in range(REACH):
                send_on(at + u, own + u).wait_send()

    edge_spreads(lambda p, copy: copy.wait_send())

    for u in range(EDGE):
        sent_edge = jnp.logical_and(sends_edges, u < out_reach)

        @pl.when(jnp.logical_and(sent_edge, has_pre))
        def _():
            send_pre(held(u), u, col - 1, 0).wait_send()

        @pl.when(jnp.logical_and(sent_edge, has_post))
        def _():
            send_post(held(tiles - 1 - u), tiles - 1 - u, col - 1, 0).wait_send()

    first_edges(lambda copy: copy.wait_send())
    store_env.wait()

    def stored(i, carry):
        store_grad(i).wait()
        return carry

    lax.fori_loop(0, tiles // 4, stored, 0)


def per_device(env_right, transfer, sources, env_left):
    ncol = lax.axis_size("col")
    nsec = lax.axis_size("sec")
    length = transfer.shape[2]
    pairs = transfer.shape[3]
    width = env_right.shape[2]
    tiles = length // TILE
    b = transfer.reshape(length * pairs, TILE)
    left = env_left.reshape(length, width)
    src = jnp.transpose(sources.reshape(tiles, pairs))
    bf16 = jnp.bfloat16
    in_hbm = pl.BlockSpec(memory_space=pltpu.HBM)
    anywhere = pl.BlockSpec(memory_space=pl.ANY)
    dma = pltpu.SemaphoreType.DMA
    env, grad = pl.pallas_call(
        functools.partial(sweep_kernel, ncol, nsec, pairs),
        out_shape=(
            jax.ShapeDtypeStruct((tiles, TILE, width), bf16),
            jax.ShapeDtypeStruct((length * pairs, TILE), bf16),
        ),
        in_specs=[in_hbm, in_hbm, in_hbm, in_hbm],
        out_specs=(anywhere, anywhere),
        scratch_shapes=[
            pltpu.SMEM((pairs, tiles), jnp.int32),
            pltpu.VMEM((length * pairs, TILE), bf16),
            pltpu.VMEM((length, pairs * TILE), bf16),
            pltpu.VMEM((length, width), bf16),
            pltpu.VMEM((length, width), bf16),
            pltpu.VMEM((tiles + 2 * EDGE, TILE, width), bf16),
            pltpu.VMEM((tiles + 2 * EDGE, TILE, width), bf16),
            pltpu.VMEM((tiles + 2 * REACH, TILE, width), bf16),
            pltpu.VMEM((length * pairs, TILE), bf16),
            pltpu.VMEM((4, pairs * TILE, TILE), jnp.float32),
            pltpu.VMEM((2 * REACH, TILE, (2 * REACH + 1) * TILE), bf16),
            pltpu.VMEM((2 * REACH, TILE, (2 * REACH + 1) * TILE), bf16),
            dma,
            dma((tiles + 2 * EDGE,)),
            dma((2 * REACH + 1 + 4 * EDGE,)),
            dma((tiles // GROUP,)),
            dma,
            dma,
            dma,
            dma((tiles // 4,)),
            dma((2 * REACH,)),
            dma((2 * REACH,)),
        ],
        compiler_params=pltpu.CompilerParams(
            collective_id=0, has_side_effects=True, vmem_limit_bytes=24 * 1024 * 1024
        ),
        name="sweep",
    )(*(pltpu.with_memory_space_constraint(x, pltpu.HBM) for x in (src, env_right.reshape(length, width), b, left)))
    return env.reshape(1, 1, length, width), grad.reshape(1, 1, length, pairs, TILE)


def solution(mesh):
    placed = (
        P(None, "sec", None),
        P("col", None, "sec", None, None),
        P("col", None, "sec", None),
        P("col", None, "sec", None),
    )
    return jax.shard_map(
        per_device,
        mesh=mesh,
        in_specs=placed,
        out_specs=(P("col", None, "sec", None), P("col", None, "sec", None, None)),
        check_vma=False,
    )
```

```python
import functools

import jax
import jax.numpy as jnp
from jax import lax
from jax.experimental import pallas as pl
from jax.experimental.pallas import tpu as pltpu
from jax.sharding import PartitionSpec as P

TILE = 128
REACH = 2
EDGE = 2 * REACH
GROUP = 4
EARLY = 3
MESH = pl.DeviceIdType.MESH


def sweep_kernel(
    ncol, nsec, pairs, src_hbm, env_hbm, b_hbm, left_hbm, env_out, grad_out,
    src_ref, b_v, a_v, left_v, env_v, land, win, fresh, grad_v, wide, spread, halo_a,
    src_sem, recv_sem, send_sem, b_sem, left_sem, env_sem, out_sem, gout_sem, spread_sem, halo_sem,
):
    col = lax.axis_index("col")
    sec = lax.axis_index("sec")
    tiles = left_v.shape[0] // TILE
    groups = tiles // GROUP
    odd = 1 - sec % 2
    first = col == ncol - 1
    wider = jnp.logical_and(col % 2 == 1, jnp.logical_not(first))
    has_below = sec > 0
    has_above = sec < nsec - 1
    side = 2 * odd - 1
    has_pre = jnp.logical_and(sec + side >= 0, sec + side < nsec)
    has_post = jnp.logical_and(sec - side >= 0, sec - side < nsec)

    def local(p):
        return p + odd * (tiles - 1 - 2 * p)

    def slot(p):
        return local(p) + EDGE

    def slot_beside(p):
        return tiles - 1 - p + odd * (2 * p + 1 - tiles) + EDGE

    def rows(t):
        return pl.ds(pl.multiple_of(t * TILE, TILE), TILE)

    def mixed(t, n=1):
        return pl.ds(pl.multiple_of(t * pairs * TILE, pairs * TILE), n * pairs * TILE)

    def load_b(g):
        span = mixed(g * GROUP, GROUP)
        return pltpu.make_async_copy(b_hbm.at[span], b_v.at[span], b_sem.at[g])

    load_src = pltpu.make_async_copy(src_hbm, src_ref, src_sem)
    load_left = pltpu.make_async_copy(left_hbm, left_v, left_sem)
    load_env = pltpu.make_async_copy(env_hbm, env_v, env_sem)
    store_env = pltpu.make_async_copy(fresh.at[pl.ds(REACH, tiles)], env_out, out_sem)

    def store_grad(i):
        span = mixed(4 * i, 4)
        return pltpu.make_async_copy(grad_v.at[span], grad_out.at[span], gout_sem.at[i])

    def send(src, w, sem, to_col, to_sec):
        return pltpu.make_async_remote_copy(
            src_ref=src,
            dst_ref=land.at[w],
            send_sem=send_sem.at[sem],
            recv_sem=recv_sem.at[w],
            device_id=(to_col, to_sec),
            device_id_type=MESH,
        )

    def held(p):
        return fresh.at[local(p) + REACH]

    def send_on(p, own=None):
        return send(held(p), slot(p), REACH if own is None else own, col - 1, sec)

    after = 2 * REACH + 1

    def send_pre(src, p, to_col, at):
        return send(src, slot_beside(-1 - p), after + at + p, to_col, sec + side)

    def send_post(src, p, to_col, at):
        return send(src, slot_beside(2 * tiles - 1 - p), after + at + EDGE + tiles - 1 - p, to_col, sec - side)

    def send_spread(h, to_sec):
        return pltpu.make_async_remote_copy(
            src_ref=spread.at[h],
            dst_ref=halo_a.at[h],
            send_sem=spread_sem.at[h],
            recv_sem=halo_sem.at[h],
            device_id=(col, to_sec),
            device_id_type=MESH,
        )

    barrier = pltpu.get_barrier_semaphore()

    def greet(to_col, to_sec):
        pl.semaphore_signal(barrier, inc=1, device_id=(to_col, to_sec), device_id_type=MESH)

    @pl.when(jnp.logical_not(first))
    def _():
        greet(col + 1, sec)

    behind = jnp.minimum(col + 1, ncol - 1)
    meets = jnp.logical_or(col % 2 == 1, col == ncol - 2)
    for there, by in ((has_below, -1), (has_above, 1)):
        @pl.when(jnp.logical_and(there, meets))
        def _():
            greet(behind, sec + by)

        @pl.when(jnp.logical_and(there, wider))
        def _():
            greet(col, sec + by)

    load_src.start()

    @pl.when(first)
    def _():
        load_env.start()

    def start_loads(i, carry):
        load_b(i + odd * (groups - 1 - 2 * i)).start()
        return carry

    lax.fori_loop(0, groups, start_loads, 0)
    load_left.start()

    def count(flag):
        return flag.astype(jnp.int32)

    beside = count(has_below) + count(has_above)

    @pl.when(col > 0)
    def _():
        pl.semaphore_wait(barrier, 1 + beside + count(first) * beside)

    def first_edges(do):
        @pl.when(jnp.logical_and(first, has_pre))
        def _():
            for u in range(REACH):
                do(send_pre(env_hbm.at[rows(local(u))], u, col, 2 * EDGE))

        @pl.when(jnp.logical_and(first, has_post))
        def _():
            for u in range(REACH):
                p = tiles - 1 - u
                do(send_post(env_hbm.at[rows(local(p))], p, col, 2 * EDGE))

    first_edges(lambda copy: copy.start())
    win[...] = jnp.zeros_like(win)
    load_src.wait()

    def sort_rows(t):
        wide[0] = b_v[mixed(t), :].astype(jnp.float32)
        for j in range(pairs):
            part = wide[0, pl.ds(j, TILE, stride=pairs), :]
            a_v[rows(t), j * TILE:(j + 1) * TILE] = part.astype(jnp.bfloat16)

    def sort_group(i):
        g = i + odd * (groups - 1 - 2 * i)
        load_b(g).wait()
        for u in range(GROUP):
            sort_rows(g * GROUP + u)

    def by_offset(t, h):
        blocks = [a_v[rows(t), j * TILE:(j + 1) * TILE].astype(jnp.float32) for j in range(pairs)]
        for k in range(2 * REACH + 1):
            total = jnp.zeros((TILE, TILE), jnp.float32)
            for j in range(pairs):
                here = src_ref[j, t] - sec * tiles - t == k - REACH
                total = total + jnp.where(here, blocks[j], 0.0)
            spread[h, :, k * TILE:(k + 1) * TILE] = total.astype(jnp.bfloat16)

    def edge_spreads(do):
        @pl.when(jnp.logical_and(wider, has_pre))
        def _():
            for u in range(REACH):
                do(u, send_spread(u, sec + side))

        @pl.when(jnp.logical_and(wider, has_post))
        def _():
            for u in range(REACH):
                do(tiles - 1 - u, send_spread(REACH + u, sec - side))

    @pl.when(jnp.logical_not(first))
    def _():
        sort_group(0)
        sort_group(groups - 1)

        @pl.when(wider)
        def _():
            for u in range(REACH):
                by_offset(local(u), u)
                by_offset(local(tiles - 1 - u), REACH + u)

        edge_spreads(lambda p, copy: copy.start())

        def one(i, carry):
            sort_group(i)
            return carry

        lax.fori_loop(1, groups - 1, one, 0)

    load_left.wait()

    def arrive(p):
        w = slot(p)
        pltpu.make_async_copy(land.at[w], land.at[w], recv_sem.at[w]).wait()
        win[w] = land[w]

    def take(p):
        @pl.when(first)
        def _():
            from_start(p)

        @pl.when(jnp.logical_not(first))
        def _():
            arrive(p)

    def picked(t):
        parts = []
        for j in range(pairs):
            i = src_ref[j, t] - sec * tiles + EDGE
            parts.append(win[jnp.clip(i, 0, win.shape[0] - 1)])
        return jnp.concatenate(parts, axis=0)

    def halo_tiles(ps, hs):
        for p, h in zip(ps, hs):
            w = slot(p)
            near = win[pl.ds(w - REACH, 2 * REACH + 1)].reshape((2 * REACH + 1) * TILE, TILE)
            acc = jnp.dot(halo_a[h], near, preferred_element_type=jnp.float32)
            fresh[local(p) + REACH] = acc.astype(jnp.bfloat16)

    def gradient(t, u):
        g = lax.dot_general(
            left_v[rows(t), :], picked(t), (((1,), (1,)), ((), ())), preferred_element_type=jnp.float32
        )
        for j in range(pairs):
            wide[u, pl.ds(j, TILE, stride=pairs), :] = g[:, j * TILE:(j + 1) * TILE]
        grad_v[mixed(t), :] = wide[u].astype(jnp.bfloat16)

    def own_tile(t):
        acc = jnp.dot(a_v[rows(t), :], picked(t), preferred_element_type=jnp.float32)
        fresh[t + REACH] = acc.astype(jnp.bfloat16)

    def from_start(p):
        win[slot(p)] = env_v[rows(local(p)), :]

    @pl.when(first)
    def _():
        load_env.wait()
        sort_group(0)
        for p in range(GROUP + REACH):
            from_start(p)
        for p in range(REACH, GROUP):
            own_tile(local(p))

    @pl.when(has_pre)
    def _():
        for u in range(REACH):
            arrive(-1 - u)

        @pl.when(wider)
        def _():
            for u in range(REACH, EDGE):
                arrive(-1 - u)

    @pl.when(jnp.logical_not(first))
    def _():
        for u in range(REACH):
            arrive(u)

    def halo_ready(hs):
        for h in hs:
            pltpu.make_async_copy(halo_a.at[h], halo_a.at[h], halo_sem.at[h]).wait()

    sends_edges = jnp.logical_and(col > 0, jnp.logical_not(wider))
    out_reach = jnp.where(first, REACH, EDGE)

    ahead_pre = jnp.logical_and(jnp.logical_and(sends_edges, has_pre), jnp.logical_not(first))
    ahead_post = jnp.logical_and(jnp.logical_and(sends_edges, has_post), jnp.logical_not(first))

    def pass_on(p):
        @pl.when(jnp.logical_and(jnp.logical_and(p < out_reach, has_pre), sends_edges))
        def _():
            send_pre(held(p), p, col - 1, 0).start()

        @pl.when(jnp.logical_and(jnp.logical_and(p >= tiles - out_reach, has_post), sends_edges))
        def _():
            send_post(held(p), p, col - 1, 0).start()

        behind_pre = jnp.logical_and(ahead_pre, p < EDGE)
        behind_post = jnp.logical_and(ahead_post, p >= tiles - EDGE)

        @pl.when(jnp.logical_and(behind_pre, p > 0))
        def _():
            send_on(p - 1).start()

        held_back = jnp.logical_or(jnp.logical_and(behind_pre, p < EDGE - 1), behind_post)

        @pl.when(jnp.logical_and(col > 0, jnp.logical_not(held_back)))
        def _():
            send_on(p).start()

    early = jnp.logical_and(wider, has_pre)
    last = tiles - REACH

    @pl.when(first)
    def _():
        for p in range(REACH):
            own_tile(local(p))
        for p in range(GROUP):
            pass_on(p)

    @pl.when(early)
    def _():
        arrive(REACH)
        halo_ready((0, 1))
        halo_tiles((-2, -1), (1, 0))
        own_tile(local(0))
        send_on(-2, 0).start()
        send_on(-1, 1).start()
        send_on(0).start()
        arrive(REACH + 1)
        arrive(REACH + 2)
        own_tile(local(1))
        own_tile(local(2))
        send_on(1).start()
        send_on(2).start()

    nearby = col < 2

    def step(p, carry):
        t = local(p)

        @pl.when(jnp.logical_and(first, p % GROUP == 0))
        def _():
            sort_group(p // GROUP)

        take(p + REACH)
        @pl.when(nearby)
        def _():
            own_tile(t)
            gradient(t, 0)

        @pl.when(jnp.logical_not(nearby))
        def _():
            own_tile(t)

        pass_on(p)

        @pl.when(jnp.logical_and(jnp.logical_and(nearby, p % GROUP == GROUP - 1), p >= GROUP))
        def _():
            store_grad(t // GROUP).start()

        return carry

    lax.fori_loop(EARLY * count(early) + GROUP * count(first), last, step, 0)

    @pl.when(has_post)
    def _():
        arrive(tiles)
        arrive(tiles + 1)

    late = jnp.logical_and(wider, has_post)

    @pl.when(late)
    def _():
        arrive(tiles + 2)
        arrive(tiles + 3)
        halo_ready((2, 3))
        own_tile(local(last))
        own_tile(local(last + 1))
        halo_tiles((tiles, tiles + 1), (2, 3))
        send_on(last).start()
        send_on(last + 1).start()
        send_on(tiles, 3).start()
        send_on(tiles + 1, 4).start()

    @pl.when(jnp.logical_not(late))
    def _():
        own_tile(local(last))
        own_tile(local(last + 1))

        @pl.when(ahead_post)
        def _():
            send_post(held(last), last, col - 1, 0).start()
            send_post(held(last + 1), last + 1, col - 1, 0).start()
            for p in range(tiles - EDGE, tiles):
                send_on(p).start()

        @pl.when(jnp.logical_not(ahead_post))
        def _():
            pass_on(last)
            pass_on(last + 1)

    store_env.start()

    @pl.when(jnp.logical_not(nearby))
    def _():
        def four(i, carry):
            for u in range(GROUP):
                gradient(GROUP * i + u, u)
            store_grad(i).start()
            return carry

        lax.fori_loop(0, groups, four, 0)

    @pl.when(nearby)
    def _():
        for u in range(EARLY):
            gradient(local(u), u)
        store_grad(local(0) // GROUP).start()
        for u in range(REACH):
            gradient(local(last + u), u)
        store_grad(local(last) // GROUP).start()

    @pl.when(col > 0)
    def _():
        main = fresh.at[pl.ds(REACH, tiles)]
        pltpu.make_async_copy(main, main, send_sem.at[REACH]).wait()

    for there, at, own in ((has_pre, -REACH, 0), (has_post, tiles, 3)):
        @pl.when(jnp.logical_and(wider, there))
        def _():
            for u in range(REACH):
                send_on(at + u, own + u).wait_send()

    edge_spreads(lambda p, copy: copy.wait_send())

    for u in range(EDGE):
        sent_edge = jnp.logical_and(sends_edges, u < out_reach)

        @pl.when(jnp.logical_and(sent_edge, has_pre))
        def _():
            send_pre(held(u), u, col - 1, 0).wait_send()

        @pl.when(jnp.logical_and(sent_edge, has_post))
        def _():
            send_post(held(tiles - 1 - u), tiles - 1 - u, col - 1, 0).wait_send()

    first_edges(lambda copy: copy.wait_send())
    store_env.wait()

    def stored(i, carry):
        store_grad(i).wait()
        return carry

    lax.fori_loop(0, tiles // 4, stored, 0)


def per_device(env_right, transfer, sources, env_left):
    ncol = lax.axis_size("col")
    nsec = lax.axis_size("sec")
    length = transfer.shape[2]
    pairs = transfer.shape[3]
    width = env_right.shape[2]
    tiles = length // TILE
    b = transfer.reshape(length * pairs, TILE)
    left = env_left.reshape(length, width)
    src = jnp.transpose(sources.reshape(tiles, pairs))
    bf16 = jnp.bfloat16
    in_hbm = pl.BlockSpec(memory_space=pltpu.HBM)
    anywhere = pl.BlockSpec(memory_space=pl.ANY)
    dma = pltpu.SemaphoreType.DMA
    env, grad = pl.pallas_call(
        functools.partial(sweep_kernel, ncol, nsec, pairs),
        out_shape=(
            jax.ShapeDtypeStruct((tiles, TILE, width), bf16),
            jax.ShapeDtypeStruct((length * pairs, TILE), bf16),
        ),
        in_specs=[in_hbm, in_hbm, in_hbm, in_hbm],
        out_specs=(anywhere, anywhere),
        scratch_shapes=[
            pltpu.SMEM((pairs, tiles), jnp.int32),
            pltpu.VMEM((length * pairs, TILE), bf16),
            pltpu.VMEM((length, pairs * TILE), bf16),
            pltpu.VMEM((length, width), bf16),
            pltpu.VMEM((length, width), bf16),
            pltpu.VMEM((tiles + 2 * EDGE, TILE, width), bf16),
            pltpu.VMEM((tiles + 2 * EDGE, TILE, width), bf16),
            pltpu.VMEM((tiles + 2 * REACH, TILE, width), bf16),
            pltpu.VMEM((length * pairs, TILE), bf16),
            pltpu.VMEM((4, pairs * TILE, TILE), jnp.float32),
            pltpu.VMEM((2 * REACH, TILE, (2 * REACH + 1) * TILE), bf16),
            pltpu.VMEM((2 * REACH, TILE, (2 * REACH + 1) * TILE), bf16),
            dma,
            dma((tiles + 2 * EDGE,)),
            dma((2 * REACH + 1 + 4 * EDGE,)),
            dma((tiles // GROUP,)),
            dma,
            dma,
            dma,
            dma((tiles // 4,)),
            dma((2 * REACH,)),
            dma((2 * REACH,)),
        ],
        compiler_params=pltpu.CompilerParams(
            collective_id=0, has_side_effects=True, vmem_limit_bytes=24 * 1024 * 1024
        ),
        name="sweep",
    )(*(pltpu.with_memory_space_constraint(x, pltpu.HBM) for x in (src, env_right.reshape(length, width), b, left)))
    return env.reshape(1, 1, length, width), grad.reshape(1, 1, length, pairs, TILE)


def solution(mesh):
    placed = (
        P(None, "sec", None),
        P("col", None, "sec", None, None),
        P("col", None, "sec", None),
        P("col", None, "sec", None),
    )
    return jax.shard_map(
        per_device,
        mesh=mesh,
        in_specs=placed,
        out_specs=(P("col", None, "sec", None), P("col", None, "sec", None, None)),
        check_vma=False,
    )
```

```python
import functools

import jax
import jax.numpy as jnp
from jax import lax
from jax.experimental import pallas as pl
from jax.experimental.pallas import tpu as pltpu
from jax.sharding import PartitionSpec as P

TILE = 128
REACH = 2
EDGE = 2 * REACH
GROUP = 4
EARLY = 3
MESH = pl.DeviceIdType.MESH


def sweep_kernel(
    ncol, nsec, pairs, src_hbm, env_hbm, b_hbm, left_hbm, env_out, grad_out,
    src_ref, b_v, a_v, left_v, env_v, land, win, fresh, grad_v, wide, spread, halo_a,
    src_sem, recv_sem, send_sem, b_sem, left_sem, env_sem, out_sem, gout_sem, spread_sem, halo_sem,
):
    col = lax.axis_index("col")
    sec = lax.axis_index("sec")
    tiles = left_v.shape[0] // TILE
    groups = tiles // GROUP
    odd = 1 - sec % 2
    first = col == ncol - 1
    wider = jnp.logical_and(col % 2 == 1, jnp.logical_not(first))
    has_below = sec > 0
    has_above = sec < nsec - 1
    side = 2 * odd - 1
    has_pre = jnp.logical_and(sec + side >= 0, sec + side < nsec)
    has_post = jnp.logical_and(sec - side >= 0, sec - side < nsec)

    def local(p):
        return p + odd * (tiles - 1 - 2 * p)

    def slot(p):
        return local(p) + EDGE

    def slot_beside(p):
        return tiles - 1 - p + odd * (2 * p + 1 - tiles) + EDGE

    def rows(t):
        return pl.ds(pl.multiple_of(t * TILE, TILE), TILE)

    def mixed(t, n=1):
        return pl.ds(pl.multiple_of(t * pairs * TILE, pairs * TILE), n * pairs * TILE)

    def load_b(g):
        span = mixed(g * GROUP, GROUP)
        return pltpu.make_async_copy(b_hbm.at[span], b_v.at[span], b_sem.at[g])

    load_src = pltpu.make_async_copy(src_hbm, src_ref, src_sem)
    load_left = pltpu.make_async_copy(left_hbm, left_v, left_sem)
    load_env = pltpu.make_async_copy(env_hbm, env_v, env_sem)
    store_env = pltpu.make_async_copy(fresh.at[pl.ds(REACH, tiles)], env_out, out_sem)

    def store_grad(i):
        span = mixed(4 * i, 4)
        return pltpu.make_async_copy(grad_v.at[span], grad_out.at[span], gout_sem.at[i])

    def send(src, w, sem, to_col, to_sec):
        return pltpu.make_async_remote_copy(
            src_ref=src,
            dst_ref=land.at[w],
            send_sem=send_sem.at[sem],
            recv_sem=recv_sem.at[w],
            device_id=(to_col, to_sec),
            device_id_type=MESH,
        )

    def held(p):
        return fresh.at[local(p) + REACH]

    def send_on(p, own=None):
        return send(held(p), slot(p), REACH if own is None else own, col - 1, sec)

    after = 2 * REACH + 1

    def send_pre(src, p, to_col, at):
        return send(src, slot_beside(-1 - p), after + at + p, to_col, sec + side)

    def send_post(src, p, to_col, at):
        return send(src, slot_beside(2 * tiles - 1 - p), after + at + EDGE + tiles - 1 - p, to_col, sec - side)

    def send_spread(h, to_sec):
        return pltpu.make_async_remote_copy(
            src_ref=spread.at[h],
            dst_ref=halo_a.at[h],
            send_sem=spread_sem.at[h],
            recv_sem=halo_sem.at[h],
            device_id=(col, to_sec),
            device_id_type=MESH,
        )

    barrier = pltpu.get_barrier_semaphore()

    def greet(to_col, to_sec):
        pl.semaphore_signal(barrier, inc=1, device_id=(to_col, to_sec), device_id_type=MESH)

    @pl.when(jnp.logical_not(first))
    def _():
        greet(col + 1, sec)

    behind = jnp.minimum(col + 1, ncol - 1)
    meets = jnp.logical_or(col % 2 == 1, col == ncol - 2)
    for there, by in ((has_below, -1), (has_above, 1)):
        @pl.when(jnp.logical_and(there, meets))
        def _():
            greet(behind, sec + by)

        @pl.when(jnp.logical_and(there, wider))
        def _():
            greet(col, sec + by)

    load_src.start()

    @pl.when(first)
    def _():
        load_env.start()

    def start_loads(i, carry):
        load_b(i + odd * (groups - 1 - 2 * i)).start()
        return carry

    lax.fori_loop(0, groups, start_loads, 0)
    load_left.start()

    def count(flag):
        return flag.astype(jnp.int32)

    beside = count(has_below) + count(has_above)

    @pl.when(col > 0)
    def _():
        pl.semaphore_wait(barrier, 1 + beside + count(first) * beside)

    def first_edges(do):
        @pl.when(jnp.logical_and(first, has_pre))
        def _():
            for u in range(REACH):
                do(send_pre(env_hbm.at[rows(local(u))], u, col, 2 * EDGE))

        @pl.when(jnp.logical_and(first, has_post))
        def _():
            for u in range(REACH):
                p = tiles - 1 - u
                do(send_post(env_hbm.at[rows(local(p))], p, col, 2 * EDGE))

    first_edges(lambda copy: copy.start())
    win[...] = jnp.zeros_like(win)
    load_src.wait()

    def sort_rows(t):
        wide[0] = b_v[mixed(t), :].astype(jnp.float32)
        for j in range(pairs):
            part = wide[0, pl.ds(j, TILE, stride=pairs), :]
            a_v[rows(t), j * TILE:(j + 1) * TILE] = part.astype(jnp.bfloat16)

    def sort_group(i):
        g = i + odd * (groups - 1 - 2 * i)
        load_b(g).wait()
        for u in range(GROUP):
            sort_rows(g * GROUP + u)

    def by_offset(t, h):
        blocks = [a_v[rows(t), j * TILE:(j + 1) * TILE].astype(jnp.float32) for j in range(pairs)]
        for k in range(2 * REACH + 1):
            total = jnp.zeros((TILE, TILE), jnp.float32)
            for j in range(pairs):
                here = src_ref[j, t] - sec * tiles - t == k - REACH
                total = total + jnp.where(here, blocks[j], 0.0)
            spread[h, :, k * TILE:(k + 1) * TILE] = total.astype(jnp.bfloat16)

    def edge_spreads(do):
        @pl.when(jnp.logical_and(wider, has_pre))
        def _():
            for u in range(REACH):
                do(u, send_spread(u, sec + side))

        @pl.when(jnp.logical_and(wider, has_post))
        def _():
            for u in range(REACH):
                do(tiles - 1 - u, send_spread(REACH + u, sec - side))

    @pl.when(jnp.logical_not(first))
    def _():
        sort_group(0)
        sort_group(groups - 1)

        @pl.when(wider)
        def _():
            for u in range(REACH):
                by_offset(local(u), u)
                by_offset(local(tiles - 1 - u), REACH + u)

        edge_spreads(lambda p, copy: copy.start())

        def one(i, carry):
            sort_group(i)
            return carry

        lax.fori_loop(1, groups - 1, one, 0)

    load_left.wait()

    def arrive(p):
        w = slot(p)
        pltpu.make_async_copy(land.at[w], land.at[w], recv_sem.at[w]).wait()
        win[w] = land[w]

    def take(p):
        @pl.when(first)
        def _():
            from_start(p)

        @pl.when(jnp.logical_not(first))
        def _():
            arrive(p)

    def picked(t):
        parts = []
        for j in range(pairs):
            i = src_ref[j, t] - sec * tiles + EDGE
            parts.append(win[jnp.clip(i, 0, win.shape[0] - 1)])
        return jnp.concatenate(parts, axis=0)

    def halo_tiles(ps, hs):
        for p, h in zip(ps, hs):
            w = slot(p)
            near = win[pl.ds(w - REACH, 2 * REACH + 1)].reshape((2 * REACH + 1) * TILE, TILE)
            acc = jnp.dot(halo_a[h], near, preferred_element_type=jnp.float32)
            fresh[local(p) + REACH] = acc.astype(jnp.bfloat16)

    def gradient(t, u):
        g = lax.dot_general(
            left_v[rows(t), :], picked(t), (((1,), (1,)), ((), ())), preferred_element_type=jnp.float32
        )
        for j in range(pairs):
            wide[u, pl.ds(j, TILE, stride=pairs), :] = g[:, j * TILE:(j + 1) * TILE]
        grad_v[mixed(t), :] = wide[u].astype(jnp.bfloat16)

    def own_tile(t):
        acc = jnp.dot(a_v[rows(t), :], picked(t), preferred_element_type=jnp.float32)
        fresh[t + REACH] = acc.astype(jnp.bfloat16)

    def from_start(p):
        win[slot(p)] = env_v[rows(local(p)), :]

    @pl.when(first)
    def _():
        load_env.wait()
        sort_group(0)
        for p in range(GROUP + REACH):
            from_start(p)
        for p in range(REACH, GROUP):
            own_tile(local(p))

    @pl.when(has_pre)
    def _():
        for u in range(REACH):
            arrive(-1 - u)

        @pl.when(wider)
        def _():
            for u in range(REACH, EDGE):
                arrive(-1 - u)

    @pl.when(jnp.logical_not(first))
    def _():
        for u in range(REACH):
            arrive(u)

    def halo_ready(hs):
        for h in hs:
            pltpu.make_async_copy(halo_a.at[h], halo_a.at[h], halo_sem.at[h]).wait()

    sends_edges = jnp.logical_and(col > 0, jnp.logical_not(wider))
    out_reach = jnp.where(first, REACH, EDGE)

    ahead_pre = jnp.logical_and(jnp.logical_and(sends_edges, has_pre), jnp.logical_not(first))
    ahead_post = jnp.logical_and(jnp.logical_and(sends_edges, has_post), jnp.logical_not(first))

    forward = col > 0

    def pass_on(p, kind):
        if kind == "first":
            if p < REACH:
                @pl.when(has_pre)
                def _():
                    send_pre(held(p), p, col - 1, 0).start()

            send_on(p).start()
            return
        before = p < EDGE
        ahead = ahead_pre if before else ahead_post

        @pl.when(ahead)
        def _():
            if before:
                send_pre(held(p), p, col - 1, 0).start()
                if p > 0:
                    send_on(p - 1).start()
                if p == EDGE - 1:
                    send_on(p).start()
            else:
                send_post(held(p), p, col - 1, 0).start()

        @pl.when(jnp.logical_and(forward, jnp.logical_not(ahead)))
        def _():
            send_on(p).start()

    early = jnp.logical_and(wider, has_pre)
    last = tiles - REACH

    @pl.when(first)
    def _():
        for p in range(REACH):
            own_tile(local(p))
        for p in range(GROUP):
            pass_on(p, "first")

    @pl.when(early)
    def _():
        arrive(REACH)
        halo_ready((0, 1))
        halo_tiles((-2, -1), (1, 0))
        own_tile(local(0))
        send_on(-2, 0).start()
        send_on(-1, 1).start()
        send_on(0).start()
        arrive(REACH + 1)
        arrive(REACH + 2)
        own_tile(local(1))
        own_tile(local(2))
        send_on(1).start()
        send_on(2).start()

    nearby = col < 2

    def advance(p, kind):
        if kind == "first":
            from_start(p + REACH)
        else:
            arrive(p + REACH)
        own_tile(local(p))
        if kind == "near":
            gradient(local(p), 0)

    def run(kind):
        def middle(p, carry):
            if kind == "first":
                @pl.when(p % GROUP == 0)
                def _():
                    sort_group(p // GROUP)

            advance(p, kind)
            if kind == "near":
                @pl.when(forward)
                def _():
                    send_on(p).start()

                @pl.when(p % GROUP == GROUP - 1)
                def _():
                    store_grad(local(p) // GROUP).start()
            else:
                send_on(p).start()
            return carry

        def head(ps):
            for p in ps:
                advance(p, kind)
                pass_on(p, kind)

        if kind != "first":
            @pl.when(jnp.logical_not(early))
            def _():
                head(range(EARLY))

            head(range(EARLY, EDGE))
            if kind == "near":
                @pl.when(jnp.logical_not(early))
                def _():
                    store_grad(local(0) // GROUP).start()

        lax.fori_loop(EDGE, tiles - EDGE, middle, 0)
        if kind == "first":
            sort_group(groups - 1)
        head(range(tiles - EDGE, last))

    @pl.when(first)
    def _():
        run("first")

    @pl.when(nearby)
    def _():
        run("near")

    @pl.when(jnp.logical_not(jnp.logical_or(first, nearby)))
    def _():
        run("plain")

    @pl.when(has_post)
    def _():
        arrive(tiles)
        arrive(tiles + 1)

    late = jnp.logical_and(wider, has_post)

    @pl.when(late)
    def _():
        arrive(tiles + 2)
        arrive(tiles + 3)
        halo_ready((2, 3))
        own_tile(local(last))
        own_tile(local(last + 1))
        halo_tiles((tiles, tiles + 1), (2, 3))
        send_on(last).start()
        send_on(last + 1).start()
        send_on(tiles, 3).start()
        send_on(tiles + 1, 4).start()

    @pl.when(jnp.logical_not(late))
    def _():
        @pl.when(nearby)
        def _():
            for u in range(REACH):
                own_tile(local(last + u))
                gradient(local(last + u), u)

        @pl.when(jnp.logical_not(nearby))
        def _():
            for u in range(REACH):
                own_tile(local(last + u))

        @pl.when(ahead_post)
        def _():
            send_post(held(last), last, col - 1, 0).start()
            send_post(held(last + 1), last + 1, col - 1, 0).start()
            for p in range(tiles - EDGE, tiles):
                send_on(p).start()

        @pl.when(jnp.logical_and(first, has_post))
        def _():
            send_post(held(last), last, col - 1, 0).start()
            send_post(held(last + 1), last + 1, col - 1, 0).start()

        @pl.when(jnp.logical_and(forward, jnp.logical_not(ahead_post)))
        def _():
            send_on(last).start()
            send_on(last + 1).start()

    @pl.when(nearby)
    def _():
        store_env.start()

    @pl.when(jnp.logical_not(nearby))
    def _():
        def four(i, carry):
            for u in range(GROUP):
                gradient(GROUP * i + u, u)
            return carry

        lax.fori_loop(0, groups, four, 0)

    @pl.when(jnp.logical_and(nearby, early))
    def _():
        for u in range(EARLY):
            gradient(local(u), u)
        store_grad(local(0) // GROUP).start()

    @pl.when(jnp.logical_and(nearby, late))
    def _():
        for u in range(REACH):
            gradient(local(last + u), u)

    @pl.when(nearby)
    def _():
        store_grad(local(last) // GROUP).start()

    @pl.when(col > 0)
    def _():
        main = fresh.at[pl.ds(REACH, tiles)]
        pltpu.make_async_copy(main, main, send_sem.at[REACH]).wait()

    for there, at, own in ((has_pre, -REACH, 0), (has_post, tiles, 3)):
        @pl.when(jnp.logical_and(wider, there))
        def _():
            for u in range(REACH):
                send_on(at + u, own + u).wait_send()

    edge_spreads(lambda p, copy: copy.wait_send())

    for u in range(EDGE):
        sent_edge = jnp.logical_and(sends_edges, u < out_reach)

        @pl.when(jnp.logical_and(sent_edge, has_pre))
        def _():
            send_pre(held(u), u, col - 1, 0).wait_send()

        @pl.when(jnp.logical_and(sent_edge, has_post))
        def _():
            send_post(held(tiles - 1 - u), tiles - 1 - u, col - 1, 0).wait_send()

    first_edges(lambda copy: copy.wait_send())

    @pl.when(jnp.logical_not(nearby))
    def _():
        store_env.start()

        def store(i, carry):
            store_grad(i).start()
            return carry

        lax.fori_loop(0, groups, store, 0)

    store_env.wait()

    def stored(i, carry):
        store_grad(i).wait()
        return carry

    lax.fori_loop(0, tiles // 4, stored, 0)


def per_device(env_right, transfer, sources, env_left):
    ncol = lax.axis_size("col")
    nsec = lax.axis_size("sec")
    length = transfer.shape[2]
    pairs = transfer.shape[3]
    width = env_right.shape[2]
    tiles = length // TILE
    b = transfer.reshape(length * pairs, TILE)
    left = env_left.reshape(length, width)
    src = jnp.transpose(sources.reshape(tiles, pairs))
    bf16 = jnp.bfloat16
    in_hbm = pl.BlockSpec(memory_space=pltpu.HBM)
    anywhere = pl.BlockSpec(memory_space=pl.ANY)
    dma = pltpu.SemaphoreType.DMA
    env, grad = pl.pallas_call(
        functools.partial(sweep_kernel, ncol, nsec, pairs),
        out_shape=(
            jax.ShapeDtypeStruct((tiles, TILE, width), bf16),
            jax.ShapeDtypeStruct((length * pairs, TILE), bf16),
        ),
        in_specs=[in_hbm, in_hbm, in_hbm, in_hbm],
        out_specs=(anywhere, anywhere),
        scratch_shapes=[
            pltpu.SMEM((pairs, tiles), jnp.int32),
            pltpu.VMEM((length * pairs, TILE), bf16),
            pltpu.VMEM((length, pairs * TILE), bf16),
            pltpu.VMEM((length, width), bf16),
            pltpu.VMEM((length, width), bf16),
            pltpu.VMEM((tiles + 2 * EDGE, TILE, width), bf16),
            pltpu.VMEM((tiles + 2 * EDGE, TILE, width), bf16),
            pltpu.VMEM((tiles + 2 * REACH, TILE, width), bf16),
            pltpu.VMEM((length * pairs, TILE), bf16),
            pltpu.VMEM((4, pairs * TILE, TILE), jnp.float32),
            pltpu.VMEM((2 * REACH, TILE, (2 * REACH + 1) * TILE), bf16),
            pltpu.VMEM((2 * REACH, TILE, (2 * REACH + 1) * TILE), bf16),
            dma,
            dma((tiles + 2 * EDGE,)),
            dma((2 * REACH + 1 + 4 * EDGE,)),
            dma((tiles // GROUP,)),
            dma,
            dma,
            dma,
            dma((tiles // 4,)),
            dma((2 * REACH,)),
            dma((2 * REACH,)),
        ],
        compiler_params=pltpu.CompilerParams(
            collective_id=0, has_side_effects=True, vmem_limit_bytes=24 * 1024 * 1024
        ),
        name="sweep",
    )(*(pltpu.with_memory_space_constraint(x, pltpu.HBM) for x in (src, env_right.reshape(length, width), b, left)))
    return env.reshape(1, 1, length, width), grad.reshape(1, 1, length, pairs, TILE)


def solution(mesh):
    placed = (
        P(None, "sec", None),
        P("col", None, "sec", None, None),
        P("col", None, "sec", None),
        P("col", None, "sec", None),
    )
    return jax.shard_map(
        per_device,
        mesh=mesh,
        in_specs=placed,
        out_specs=(P("col", None, "sec", None), P("col", None, "sec", None, None)),
        check_vma=False,
    )
```

```python
import functools

import jax
import jax.numpy as jnp
from jax import lax
from jax.experimental import pallas as pl
from jax.experimental.pallas import tpu as pltpu
from jax.sharding import PartitionSpec as P

TILE = 128
REACH = 2
EDGE = 2 * REACH
GROUP = 4
EARLY = 3
MESH = pl.DeviceIdType.MESH


def sweep_kernel(
    ncol, nsec, pairs, src_hbm, env_hbm, b_hbm, left_hbm, env_out, grad_out,
    src_ref, b_v, a_v, left_v, env_v, land, win, fresh, grad_v, wide, spread, halo_a,
    src_sem, recv_sem, send_sem, b_sem, left_sem, env_sem, out_sem, gout_sem, spread_sem, halo_sem,
):
    col = lax.axis_index("col")
    sec = lax.axis_index("sec")
    tiles = left_v.shape[0] // TILE
    groups = tiles // GROUP
    odd = 1 - sec % 2
    first = col == ncol - 1
    wider = jnp.logical_and(col % 2 == 1, jnp.logical_not(first))
    has_below = sec > 0
    has_above = sec < nsec - 1
    side = 2 * odd - 1
    has_pre = jnp.logical_and(sec + side >= 0, sec + side < nsec)
    has_post = jnp.logical_and(sec - side >= 0, sec - side < nsec)

    def local(p):
        return p + odd * (tiles - 1 - 2 * p)

    def slot(p):
        return local(p) + EDGE

    def slot_beside(p):
        return tiles - 1 - p + odd * (2 * p + 1 - tiles) + EDGE

    def rows(t):
        return pl.ds(pl.multiple_of(t * TILE, TILE), TILE)

    def mixed(t, n=1):
        return pl.ds(pl.multiple_of(t * pairs * TILE, pairs * TILE), n * pairs * TILE)

    def load_b(g):
        span = mixed(g * GROUP, GROUP)
        return pltpu.make_async_copy(b_hbm.at[span], b_v.at[span], b_sem.at[g])

    load_src = pltpu.make_async_copy(src_hbm, src_ref, src_sem)
    load_left = pltpu.make_async_copy(left_hbm, left_v, left_sem)
    load_env = pltpu.make_async_copy(env_hbm, env_v, env_sem)
    store_env = pltpu.make_async_copy(fresh.at[pl.ds(REACH, tiles)], env_out, out_sem)

    def store_grad(i):
        span = mixed(4 * i, 4)
        return pltpu.make_async_copy(grad_v.at[span], grad_out.at[span], gout_sem.at[i])

    def send(src, w, sem, to_col, to_sec):
        return pltpu.make_async_remote_copy(
            src_ref=src,
            dst_ref=land.at[w],
            send_sem=send_sem.at[sem],
            recv_sem=recv_sem.at[w],
            device_id=(to_col, to_sec),
            device_id_type=MESH,
        )

    def held(p):
        return fresh.at[local(p) + REACH]

    def send_on(p, own=None):
        return send(held(p), slot(p), REACH if own is None else own, col - 1, sec)

    after = 2 * REACH + 1

    def send_pre(src, p, to_col, at):
        return send(src, slot_beside(-1 - p), after + at + p, to_col, sec + side)

    def send_post(src, p, to_col, at):
        return send(src, slot_beside(2 * tiles - 1 - p), after + at + EDGE + tiles - 1 - p, to_col, sec - side)

    def send_spread(h, to_sec):
        return pltpu.make_async_remote_copy(
            src_ref=spread.at[h],
            dst_ref=halo_a.at[h],
            send_sem=spread_sem.at[h],
            recv_sem=halo_sem.at[h],
            device_id=(col, to_sec),
            device_id_type=MESH,
        )

    barrier = pltpu.get_barrier_semaphore()

    def greet(to_col, to_sec):
        pl.semaphore_signal(barrier, inc=1, device_id=(to_col, to_sec), device_id_type=MESH)

    @pl.when(jnp.logical_not(first))
    def _():
        greet(col + 1, sec)

    behind = jnp.minimum(col + 1, ncol - 1)
    meets = jnp.logical_or(col % 2 == 1, col == ncol - 2)
    for there, by in ((has_below, -1), (has_above, 1)):
        @pl.when(jnp.logical_and(there, meets))
        def _():
            greet(behind, sec + by)

        @pl.when(jnp.logical_and(there, wider))
        def _():
            greet(col, sec + by)

    load_src.start()

    @pl.when(first)
    def _():
        load_env.start()

    def start_loads(i, carry):
        load_b(i + odd * (groups - 1 - 2 * i)).start()
        return carry

    lax.fori_loop(0, groups, start_loads, 0)
    load_left.start()

    def count(flag):
        return flag.astype(jnp.int32)

    beside = count(has_below) + count(has_above)

    @pl.when(col > 0)
    def _():
        pl.semaphore_wait(barrier, 1 + beside + count(first) * beside)

    def first_edges(do):
        @pl.when(jnp.logical_and(first, has_pre))
        def _():
            for u in range(REACH):
                do(send_pre(env_hbm.at[rows(local(u))], u, col, 2 * EDGE))

        @pl.when(jnp.logical_and(first, has_post))
        def _():
            for u in range(REACH):
                p = tiles - 1 - u
                do(send_post(env_hbm.at[rows(local(p))], p, col, 2 * EDGE))

    first_edges(lambda copy: copy.start())
    win[...] = jnp.zeros_like(win)
    load_src.wait()

    def sort_rows(t):
        wide[0] = b_v[mixed(t), :].astype(jnp.float32)
        for j in range(pairs):
            part = wide[0, pl.ds(j, TILE, stride=pairs), :]
            a_v[rows(t), j * TILE:(j + 1) * TILE] = part.astype(jnp.bfloat16)

    def sort_group(i):
        g = i + odd * (groups - 1 - 2 * i)
        load_b(g).wait()
        for u in range(GROUP):
            sort_rows(g * GROUP + u)

    def by_offset(t, h):
        blocks = [a_v[rows(t), j * TILE:(j + 1) * TILE].astype(jnp.float32) for j in range(pairs)]
        for k in range(2 * REACH + 1):
            total = jnp.zeros((TILE, TILE), jnp.float32)
            for j in range(pairs):
                here = src_ref[j, t] - sec * tiles - t == k - REACH
                total = total + jnp.where(here, blocks[j], 0.0)
            spread[h, :, k * TILE:(k + 1) * TILE] = total.astype(jnp.bfloat16)

    def edge_spreads(do):
        @pl.when(jnp.logical_and(wider, has_pre))
        def _():
            for u in range(REACH):
                do(u, send_spread(u, sec + side))

        @pl.when(jnp.logical_and(wider, has_post))
        def _():
            for u in range(REACH):
                do(tiles - 1 - u, send_spread(REACH + u, sec - side))

    @pl.when(jnp.logical_not(first))
    def _():
        sort_group(0)
        sort_group(groups - 1)

        @pl.when(wider)
        def _():
            for u in range(REACH):
                by_offset(local(u), u)
                by_offset(local(tiles - 1 - u), REACH + u)

        edge_spreads(lambda p, copy: copy.start())

        def one(i, carry):
            sort_group(i)
            return carry

        lax.fori_loop(1, groups - 1, one, 0)

    load_left.wait()

    def arrive(p):
        w = slot(p)
        pltpu.make_async_copy(land.at[w], land.at[w], recv_sem.at[w]).wait()
        win[w] = land[w]

    def take(p):
        @pl.when(first)
        def _():
            from_start(p)

        @pl.when(jnp.logical_not(first))
        def _():
            arrive(p)

    def picked(t):
        parts = []
        for j in range(pairs):
            i = src_ref[j, t] - sec * tiles + EDGE
            parts.append(win[jnp.clip(i, 0, win.shape[0] - 1)])
        return jnp.concatenate(parts, axis=0)

    def halo_tiles(ps, hs):
        for p, h in zip(ps, hs):
            w = slot(p)
            near = win[pl.ds(w - REACH, 2 * REACH + 1)].reshape((2 * REACH + 1) * TILE, TILE)
            acc = jnp.dot(halo_a[h], near, preferred_element_type=jnp.float32)
            fresh[local(p) + REACH] = acc.astype(jnp.bfloat16)

    def gradient(t, u):
        g = lax.dot_general(
            left_v[rows(t), :], picked(t), (((1,), (1,)), ((), ())), preferred_element_type=jnp.float32
        )
        for j in range(pairs):
            wide[u, pl.ds(j, TILE, stride=pairs), :] = g[:, j * TILE:(j + 1) * TILE]
        grad_v[mixed(t), :] = wide[u].astype(jnp.bfloat16)

    def own_tile(t):
        acc = jnp.dot(a_v[rows(t), :], picked(t), preferred_element_type=jnp.float32)
        fresh[t + REACH] = acc.astype(jnp.bfloat16)

    def from_start(p):
        win[slot(p)] = env_v[rows(local(p)), :]

    @pl.when(first)
    def _():
        load_env.wait()
        sort_group(0)
        for p in range(GROUP + REACH):
            from_start(p)
        for p in range(REACH, GROUP):
            own_tile(local(p))

    @pl.when(has_pre)
    def _():
        for u in range(REACH):
            arrive(-1 - u)

        @pl.when(wider)
        def _():
            for u in range(REACH, EDGE):
                arrive(-1 - u)

    @pl.when(jnp.logical_not(first))
    def _():
        for u in range(REACH):
            arrive(u)

    def halo_ready(hs):
        for h in hs:
            pltpu.make_async_copy(halo_a.at[h], halo_a.at[h], halo_sem.at[h]).wait()

    sends_edges = jnp.logical_and(col > 0, jnp.logical_not(wider))
    out_reach = jnp.where(first, REACH, EDGE)

    ahead_pre = jnp.logical_and(jnp.logical_and(sends_edges, has_pre), jnp.logical_not(first))
    ahead_post = jnp.logical_and(jnp.logical_and(sends_edges, has_post), jnp.logical_not(first))

    forward = col > 0

    def pass_on(p, kind):
        if kind == "first":
            if p < REACH:
                @pl.when(has_pre)
                def _():
                    send_pre(held(p), p, col - 1, 0).start()

            send_on(p).start()
            return
        before = p < EDGE
        ahead = ahead_pre if before else ahead_post

        @pl.when(ahead)
        def _():
            if before:
                send_pre(held(p), p, col - 1, 0).start()
                if p > 0:
                    send_on(p - 1).start()
                if p == EDGE - 1:
                    send_on(p).start()
            else:
                send_post(held(p), p, col - 1, 0).start()

        @pl.when(jnp.logical_and(forward, jnp.logical_not(ahead)))
        def _():
            send_on(p).start()

    early = jnp.logical_and(wider, has_pre)
    last = tiles - REACH

    @pl.when(first)
    def _():
        for p in range(REACH):
            own_tile(local(p))
        for p in range(GROUP):
            pass_on(p, "first")

    @pl.when(early)
    def _():
        arrive(REACH)
        halo_ready((0, 1))
        halo_tiles((-2, -1), (1, 0))
        own_tile(local(0))
        send_on(-2, 0).start()
        send_on(-1, 1).start()
        send_on(0).start()
        arrive(REACH + 1)
        arrive(REACH + 2)
        own_tile(local(1))
        own_tile(local(2))
        send_on(1).start()
        send_on(2).start()

    nearby = col < 2

    def advance(p, kind):
        if kind == "first":
            from_start(p + REACH)
        else:
            arrive(p + REACH)
        own_tile(local(p))
        if kind == "near":
            gradient(local(p), 0)

    def run(kind):
        def middle(p, carry):
            if kind == "first":
                @pl.when(p % GROUP == 0)
                def _():
                    sort_group(p // GROUP)

            advance(p, kind)
            if kind == "near":
                @pl.when(forward)
                def _():
                    send_on(p).start()

                @pl.when(p % GROUP == GROUP - 1)
                def _():
                    store_grad(local(p) // GROUP).start()
            else:
                send_on(p).start()
            return carry

        def head(ps):
            for p in ps:
                advance(p, kind)
                pass_on(p, kind)

        if kind != "first":
            @pl.when(jnp.logical_not(early))
            def _():
                head(range(EARLY))

            head(range(EARLY, EDGE))
            if kind == "near":
                @pl.when(jnp.logical_not(early))
                def _():
                    store_grad(local(0) // GROUP).start()

        lax.fori_loop(EDGE, tiles - EDGE, middle, 0)
        if kind == "first":
            sort_group(groups - 1)
        if kind == "near":
            @pl.when(forward)
            def _():
                head(range(tiles - EDGE, last))
        else:
            head(range(tiles - EDGE, last))

    @pl.when(first)
    def _():
        run("first")

    @pl.when(nearby)
    def _():
        run("near")

    @pl.when(jnp.logical_not(jnp.logical_or(first, nearby)))
    def _():
        run("plain")

    @pl.when(col == 0)
    def _():
        arrive(last)
        arrive(last + 1)

    @pl.when(has_post)
    def _():
        arrive(tiles)
        arrive(tiles + 1)

    late = jnp.logical_and(wider, has_post)

    @pl.when(late)
    def _():
        arrive(tiles + 2)
        arrive(tiles + 3)
        halo_ready((2, 3))
        own_tile(local(last))
        own_tile(local(last + 1))
        halo_tiles((tiles, tiles + 1), (2, 3))
        send_on(last).start()
        send_on(last + 1).start()
        send_on(tiles, 3).start()
        send_on(tiles + 1, 4).start()

    @pl.when(jnp.logical_not(late))
    def _():
        @pl.when(col == 0)
        def _():
            for u in range(EDGE):
                own_tile(local(tiles - EDGE + u))
                gradient(local(tiles - EDGE + u), u)

        @pl.when(col == 1)
        def _():
            for u in range(REACH):
                own_tile(local(last + u))
                gradient(local(last + u), u)

        @pl.when(jnp.logical_not(nearby))
        def _():
            for u in range(REACH):
                own_tile(local(last + u))

        @pl.when(ahead_post)
        def _():
            send_post(held(last), last, col - 1, 0).start()
            send_post(held(last + 1), last + 1, col - 1, 0).start()
            for p in range(tiles - EDGE, tiles):
                send_on(p).start()

        @pl.when(jnp.logical_and(first, has_post))
        def _():
            send_post(held(last), last, col - 1, 0).start()
            send_post(held(last + 1), last + 1, col - 1, 0).start()

        @pl.when(jnp.logical_and(forward, jnp.logical_not(ahead_post)))
        def _():
            send_on(last).start()
            send_on(last + 1).start()

    @pl.when(nearby)
    def _():
        store_env.start()

    @pl.when(jnp.logical_not(nearby))
    def _():
        def four(i, carry):
            for u in range(GROUP):
                gradient(GROUP * i + u, u)
            return carry

        lax.fori_loop(0, groups, four, 0)

    @pl.when(jnp.logical_and(nearby, early))
    def _():
        for u in range(EARLY):
            gradient(local(u), u)
        store_grad(local(0) // GROUP).start()

    @pl.when(jnp.logical_and(nearby, late))
    def _():
        for u in range(REACH):
            gradient(local(last + u), u)

    @pl.when(nearby)
    def _():
        store_grad(local(last) // GROUP).start()

    @pl.when(col > 0)
    def _():
        main = fresh.at[pl.ds(REACH, tiles)]
        pltpu.make_async_copy(main, main, send_sem.at[REACH]).wait()

    for there, at, own in ((has_pre, -REACH, 0), (has_post, tiles, 3)):
        @pl.when(jnp.logical_and(wider, there))
        def _():
            for u in range(REACH):
                send_on(at + u, own + u).wait_send()

    edge_spreads(lambda p, copy: copy.wait_send())

    for u in range(EDGE):
        sent_edge = jnp.logical_and(sends_edges, u < out_reach)

        @pl.when(jnp.logical_and(sent_edge, has_pre))
        def _():
            send_pre(held(u), u, col - 1, 0).wait_send()

        @pl.when(jnp.logical_and(sent_edge, has_post))
        def _():
            send_post(held(tiles - 1 - u), tiles - 1 - u, col - 1, 0).wait_send()

    first_edges(lambda copy: copy.wait_send())

    @pl.when(jnp.logical_not(nearby))
    def _():
        store_env.start()

        def store(i, carry):
            store_grad(i).start()
            return carry

        lax.fori_loop(0, groups, store, 0)

    store_env.wait()

    def stored(i, carry):
        store_grad(i).wait()
        return carry

    lax.fori_loop(0, tiles // 4, stored, 0)


def per_device(env_right, transfer, sources, env_left):
    ncol = lax.axis_size("col")
    nsec = lax.axis_size("sec")
    length = transfer.shape[2]
    pairs = transfer.shape[3]
    width = env_right.shape[2]
    tiles = length // TILE
    b = transfer.reshape(length * pairs, TILE)
    left = env_left.reshape(length, width)
    src = jnp.transpose(sources.reshape(tiles, pairs))
    bf16 = jnp.bfloat16
    in_hbm = pl.BlockSpec(memory_space=pltpu.HBM)
    anywhere = pl.BlockSpec(memory_space=pl.ANY)
    dma = pltpu.SemaphoreType.DMA
    env, grad = pl.pallas_call(
        functools.partial(sweep_kernel, ncol, nsec, pairs),
        out_shape=(
            jax.ShapeDtypeStruct((tiles, TILE, width), bf16),
            jax.ShapeDtypeStruct((length * pairs, TILE), bf16),
        ),
        in_specs=[in_hbm, in_hbm, in_hbm, in_hbm],
        out_specs=(anywhere, anywhere),
        scratch_shapes=[
            pltpu.SMEM((pairs, tiles), jnp.int32),
            pltpu.VMEM((length * pairs, TILE), bf16),
            pltpu.VMEM((length, pairs * TILE), bf16),
            pltpu.VMEM((length, width), bf16),
            pltpu.VMEM((length, width), bf16),
            pltpu.VMEM((tiles + 2 * EDGE, TILE, width), bf16),
            pltpu.VMEM((tiles + 2 * EDGE, TILE, width), bf16),
            pltpu.VMEM((tiles + 2 * REACH, TILE, width), bf16),
            pltpu.VMEM((length * pairs, TILE), bf16),
            pltpu.VMEM((4, pairs * TILE, TILE), jnp.float32),
            pltpu.VMEM((2 * REACH, TILE, (2 * REACH + 1) * TILE), bf16),
            pltpu.VMEM((2 * REACH, TILE, (2 * REACH + 1) * TILE), bf16),
            dma,
            dma((tiles + 2 * EDGE,)),
            dma((2 * REACH + 1 + 4 * EDGE,)),
            dma((tiles // GROUP,)),
            dma,
            dma,
            dma,
            dma((tiles // 4,)),
            dma((2 * REACH,)),
            dma((2 * REACH,)),
        ],
        compiler_params=pltpu.CompilerParams(
            collective_id=0, has_side_effects=True, vmem_limit_bytes=24 * 1024 * 1024
        ),
        name="sweep",
    )(*(pltpu.with_memory_space_constraint(x, pltpu.HBM) for x in (src, env_right.reshape(length, width), b, left)))
    return env.reshape(1, 1, length, width), grad.reshape(1, 1, length, pairs, TILE)


def solution(mesh):
    placed = (
        P(None, "sec", None),
        P("col", None, "sec", None, None),
        P("col", None, "sec", None),
        P("col", None, "sec", None),
    )
    return jax.shard_map(
        per_device,
        mesh=mesh,
        in_specs=placed,
        out_specs=(P("col", None, "sec", None), P("col", None, "sec", None, None)),
        check_vma=False,
    )
```
